32 devices in a mesh: groups: 2 (over y), seq: 4 (over z), head: 2 (over x), section: 2 (over core).
Axes of the slice: x: 2, y: 2, z: 4, core: 2. Of those that a mesh axis runs over, the one named last changes fastest.
Arguments:
- q_heads: bfloat16 [2, 1024, 12288], P('section', ('groups', 'seq'), 'head'), parts along dimension 1, may hold values from -256 to 256
- cache_latent: bfloat16 [2, 1024, 512], P('section', ('groups', 'seq')), parts along dimension 1, may hold values from -6 to 6
- cache_rope: bfloat16 [2, 1024, 64], P('section', ('groups', 'seq')), parts along dimension 1, may hold values from -6.5 to 6.5
- span_start: int32 [2, 4], P('section', 'groups'), parts along dimension 1, may hold values from 1 to 256, as said below
- prefix_len: int32 [2, 4], P('section', 'groups'), parts along dimension 1, may hold values from 0 to 256, as said below
- key_up: bfloat16 [2, 64, 128, 512], P('section', 'head'), may hold values from -0.5 to 0.5
- value_up: bfloat16 [2, 64, 512, 128], P('section', 'head'), may hold values from -2 to 2
- out_weight: bfloat16 [2, 8192, 7168], P('section', 'head', 'seq'), may hold values from -0.0625 to 0.0625
Outputs:
- mixed_out: bfloat16 [2, 1024, 7168], P('section', ('groups', 'head'), 'seq'), parts along dimension 1
The draws below stay inside these ranges and needn't reach their ends.
There are 2 independent parts, one for each index of `groups`. The reference program is written for one: setup_inputs(seed, part) draws one part's arguments, and reference() takes and returns one part's arrays. A program takes and returns all parts, laid end to end along the dimension named above; an argument that names none is the same for every part. Nothing has to cross between parts.
Inputs may be any that keep to these rules, and one draw needn't show every extreme that they name: Span j's own tokens are context positions span_start to span_start + 255; the last span of every layer starts at 256. `prefix_len`: below the span's span_start for every span but the last; equal to it for the last span of every layer.
All inputs are finite; a program needn't handle non-finite values.
Results may differ from the reference program's by a relative error of at most 0.0085.
Values may be sent and summed in bfloat16 or wider, within the bound.
No kernel may reach another device: no remote copies, remote signals or barrier semaphores. Data moves between devices by JAX's collectives and lax.ppermute only.
A program may use at most 64 MiB of HBM per device.

```python
import jax
import jax.numpy as jnp
from jax import lax

D = 7168
HEADS = 64
NOPE = 128
ROPE = 64
LAT = 512
VDIM = 128
NSPAN = 2
LAYERS = 2
QT = 512
CTX = 512
SPAN = 256


def span_layout(key):
    first_key, second_key = jax.random.split(jax.random.fold_in(key, 11))
    last_start = CTX - SPAN
    grid_shape = (LAYERS, NSPAN)
    is_last = jnp.arange(NSPAN)[None, :] == NSPAN - 1
    drawn_first = jax.random.randint(first_key, grid_shape, 1, last_start + 1)
    span_first = jnp.where(is_last, last_start, drawn_first)
    drawn_prefix = jax.random.randint(second_key, grid_shape, 0, jnp.maximum(span_first, 1))
    prefix_row = jnp.where(is_last, span_first, drawn_prefix)
    return (span_first.astype(jnp.int32), prefix_row.astype(jnp.int32))


def draw_span_start(key, part):
    return span_layout(key)[0]


def draw_prefix_len(key, part):
    return span_layout(key)[1]


def draw_cache_rope(key, part):
    drawn = jnp.clip(jax.random.normal(jax.random.fold_in(key, 21), (LAYERS, CTX, ROPE), jnp.float32), -6.0, 6.0)
    return drawn.astype(jnp.bfloat16)


def draw_q_heads(key, part):
    width_all = NOPE + ROPE
    drawn = jnp.clip(jax.random.normal(jax.random.fold_in(key, 31), (LAYERS, QT, HEADS, width_all), jnp.float32), -6.0, 6.0)
    return drawn.reshape(LAYERS, QT, HEADS * width_all).astype(jnp.bfloat16)


def steps_of(key, extent, cuts, smallest, top_value):
    factor_of = 1.0
    for position, blocks in cuts:
        draws = jax.random.uniform(jax.random.fold_in(jax.random.fold_in(key, 6), position), (blocks,), jnp.float32, smallest / len(cuts), top_value / len(cuts))
        factor_of = factor_of * jnp.repeat(jnp.exp(draws), extent[position] // blocks).reshape((-1,) + (1,) * (len(extent) - 1 - position))
    return factor_of


def normal_values(key, shape, deviation, reach, shards=(), kind=jnp.bfloat16):
    array = deviation * jax.random.normal(key, shape, jnp.float32)
    if shards:
        array = array * steps_of(key, shape, shards, -0.22, 0.18)
    return jnp.clip(array, -reach, reach).astype(kind)


def setup_inputs(seed: int = 0, part: int = 0) -> dict:
    arg_keys = jax.random.split(jax.random.key(seed), 9)
    part_keys = jax.random.split(jax.random.fold_in(arg_keys[8], part), 9)
    q_heads = draw_q_heads(jax.random.fold_in(jax.random.fold_in(arg_keys[8], part), 71), part)
    cache_latent = normal_values(part_keys[1], (LAYERS, CTX, LAT), 1.0, 6.0, ((0, 2), (1, 4)))
    cache_rope = draw_cache_rope(jax.random.fold_in(jax.random.fold_in(arg_keys[8], part), 71), part)
    span_start = draw_span_start(jax.random.fold_in(jax.random.fold_in(arg_keys[8], part), 71), part)
    prefix_len = draw_prefix_len(jax.random.fold_in(jax.random.fold_in(arg_keys[8], part), 71), part)
    key_up = normal_values(arg_keys[5], (LAYERS, HEADS, NOPE, LAT), NOPE ** -0.5, 0.5, ((0, 2), (1, 2)))
    value_up = normal_values(arg_keys[6], (LAYERS, HEADS, LAT, VDIM), 0.15, 2.0, ((0, 2), (1, 2)))
    out_weight = normal_values(arg_keys[7], (LAYERS, HEADS * VDIM, D), (HEADS * VDIM) ** -0.5, 0.0625, ((0, 2), (1, 2), (2, 4)))
    return {"q_heads": q_heads, "cache_latent": cache_latent, "cache_rope": cache_rope, "span_start": span_start, "prefix_len": prefix_len, "key_up": key_up, "value_up": value_up, "out_weight": out_weight}


def reference(q_heads, cache_latent, cache_rope, span_start, prefix_len, key_up, value_up, out_weight):
    softmax_scale = (NOPE + ROPE) ** -0.5
    token_ids = jnp.arange(QT, dtype=jnp.int32)
    span_ids = token_ids // SPAN
    in_span = token_ids % SPAN
    key_pos = jnp.arange(CTX, dtype=jnp.int32)
    results = []
    for layer_idx in range(LAYERS):
        span_first = span_start[layer_idx][span_ids]
        prefix_row = prefix_len[layer_idx][span_ids]
        positions = span_first + in_span
        visible = (key_pos[None, :] < prefix_row[:, None]) | ((key_pos[None, :] >= span_first[:, None]) & (key_pos[None, :] <= positions[:, None]))
        queries = q_heads[layer_idx].reshape(QT, HEADS, NOPE + ROPE)
        latent = cache_latent[layer_idx]
        rope_keys = cache_rope[layer_idx]

        def one_head(inputs):
            query_head, key_map, value_map = inputs
            absorbed = jnp.dot(query_head[:, :NOPE], key_map, preferred_element_type=jnp.float32).astype(jnp.bfloat16)
            scores = (jnp.dot(absorbed, latent.T, preferred_element_type=jnp.float32) + jnp.dot(query_head[:, NOPE:], rope_keys.T, preferred_element_type=jnp.float32)) * softmax_scale
            scores = jnp.where(visible, scores, -jnp.inf)
            peak_score = jnp.max(scores, axis=1, keepdims=True)
            weights = jnp.where(visible, jnp.exp(scores - peak_score), 0.0)
            row_total = jnp.sum(weights, axis=1, keepdims=True)
            rounded = weights.astype(jnp.bfloat16)
            latent_out = (jnp.dot(rounded, latent, preferred_element_type=jnp.float32) / row_total).astype(jnp.bfloat16)
            return jnp.dot(latent_out, value_map, preferred_element_type=jnp.float32).astype(jnp.bfloat16)

        head_outs = lax.map(one_head, (jnp.swapaxes(queries, 0, 1), key_up[layer_idx], value_up[layer_idx]))
        joined = jnp.swapaxes(head_outs, 0, 1).reshape(QT, HEADS * VDIM)
        results.append(jnp.dot(joined, out_weight[layer_idx], preferred_element_type=jnp.float32).astype(jnp.bfloat16))
    return jnp.stack(results)
```

```python
import functools

import jax
import jax.numpy as jnp
from jax import lax
from jax.experimental import pallas as pl
from jax.experimental.pallas import tpu as pltpu
from jax.sharding import PartitionSpec as P

NSPAN = 2
LANES = 128
ROWS = 16

masked_fill = -1e30


def exchange(value, axis, distance):
    count = lax.axis_size(axis)
    return lax.ppermute(value, axis, [(i, i ^ distance) for i in range(count)])


def absorb_kernel(query_ref, key_up_ref, out_ref, *, nope_dim, rope_dim):
    heads = key_up_ref.shape[0]
    lat_dim = key_up_ref.shape[2]
    tokens = query_ref.shape[0]
    pair_width = 2 * (nope_dim + rope_dim)
    lane = lax.broadcasted_iota(jnp.int32, (tokens, 2 * rope_dim), 1)
    for pair in range(heads // 2):
        base = pair * pair_width
        even_nope = query_ref[:, base : base + nope_dim]
        even_rope = query_ref[:, base + nope_dim : base + nope_dim + 2 * rope_dim]
        odd_all = query_ref[:, base + nope_dim : base + pair_width]
        odd_rope = query_ref[:, base + pair_width - 2 * rope_dim : base + pair_width]
        pad = jnp.zeros((rope_dim, lat_dim), key_up_ref.dtype)
        odd_map = jnp.concatenate([pad, key_up_ref[2 * pair + 1], pad], axis=0)
        out_ref[2 * pair, :, :lat_dim] = jnp.dot(
            even_nope, key_up_ref[2 * pair], preferred_element_type=jnp.float32
        ).astype(out_ref.dtype)
        out_ref[2 * pair + 1, :, :lat_dim] = jnp.dot(
            odd_all, odd_map, preferred_element_type=jnp.float32
        ).astype(out_ref.dtype)
        zero = jnp.zeros_like(even_rope)
        out_ref[2 * pair, :, lat_dim:] = jnp.where(lane < rope_dim, even_rope, zero)
        out_ref[2 * pair + 1, :, lat_dim:] = jnp.where(lane >= rope_dim, odd_rope, zero)


def absorb(queries, key_up, rope_dim, head_block):
    tokens = queries.shape[0]
    heads, nope_dim, lat_dim = key_up.shape
    head_width = nope_dim + rope_dim
    out_dim = lat_dim + 2 * rope_dim
    return pl.pallas_call(
        functools.partial(absorb_kernel, nope_dim=nope_dim, rope_dim=rope_dim),
        grid=(heads // head_block,),
        in_specs=[
            pl.BlockSpec((tokens, head_block * head_width), lambda i: (0, i)),
            pl.BlockSpec((head_block, nope_dim, lat_dim), lambda i: (i, 0, 0)),
        ],
        out_specs=pl.BlockSpec((head_block, tokens, out_dim), lambda i: (i, 0, 0)),
        out_shape=jax.ShapeDtypeStruct((heads, tokens, out_dim), queries.dtype),
        compiler_params=pltpu.CompilerParams(vmem_limit_bytes=24 << 20),
        cost_estimate=pl.CostEstimate(
            flops=2 * tokens * heads * nope_dim * lat_dim,
            bytes_accessed=2 * (queries.size + key_up.size + heads * tokens * out_dim),
            transcendentals=0,
        ),
    )(queries, key_up)


def attend_kernel(
    scalars_ref, query_ref, own_ref, near_ref, far_ref, cross_ref, value_up_ref, out_ref,
    keys_ref, keys_t_ref, hide_ref, *, softmax_scale, lat_dim, first_token,
):
    heads, tokens, width = query_ref.shape
    block = own_ref.shape[0]
    context = keys_ref.shape[0]

    @pl.when(pl.program_id(0) == 0)
    def _():
        for slot, ref in enumerate((own_ref, near_ref, far_ref, cross_ref)):
            keys_ref[slot * block : (slot + 1) * block, :] = ref[...]
        keys_t_ref[...] = keys_ref[...].T
        here = scalars_ref[0]
        span_first = scalars_ref[2]
        prefix = scalars_ref[3]
        first_pos = scalars_ref[4] + first_token
        column = lax.broadcasted_iota(jnp.int32, (tokens, context), 1)
        row = lax.broadcasted_iota(jnp.int32, (tokens, context), 0)
        position = lax.bitwise_xor(column // block, here) * block + column % block
        visible = (position < prefix) | (
            (position >= span_first) & (position <= row + first_pos)
        )
        hide_ref[...] = jnp.where(visible, 0.0, masked_fill)

    query = query_ref[...].reshape(heads * tokens, width)
    scores = jnp.dot(query, keys_t_ref[...], preferred_element_type=jnp.float32)
    scores = scores.reshape(heads, tokens, context) + hide_ref[...][None]
    peak = jnp.max(scores, axis=2, keepdims=True)
    weights = jnp.exp((scores - peak) * softmax_scale)
    inverse = 1.0 / jnp.sum(weights, axis=2, keepdims=True)
    rounded = weights.astype(keys_ref.dtype).reshape(heads * tokens, context)
    summed = jnp.dot(rounded, keys_ref[:, :lat_dim], preferred_element_type=jnp.float32)
    latent_out = (summed.reshape(heads, tokens, lat_dim) * inverse).astype(keys_ref.dtype)
    value_dim = value_up_ref.shape[2]
    for head in range(heads):
        out_ref[:, head * value_dim : (head + 1) * value_dim] = jnp.dot(
            latent_out[head], value_up_ref[head], preferred_element_type=jnp.float32
        ).astype(out_ref.dtype)


def attend(scalars, absorbed, slots, value_up, softmax_scale, first_token, tokens, head_block):
    heads, _, width = absorbed.shape
    _, lat_dim, value_dim = value_up.shape
    block = slots[0].shape[0]
    context = block * len(slots)
    step = first_token // tokens if first_token % tokens == 0 else None
    slot_spec = pl.BlockSpec((block, width), lambda i, s: (0, 0))
    query_spec = pl.BlockSpec(
        (head_block, pl.Element(tokens), width), lambda i, s: (i, first_token, 0)
    )
    if step is not None:
        query_spec = pl.BlockSpec((head_block, tokens, width), lambda i, s: (i, step, 0))
    return pl.pallas_call(
        functools.partial(
            attend_kernel, softmax_scale=softmax_scale, lat_dim=lat_dim, first_token=first_token
        ),
        grid_spec=pltpu.PrefetchScalarGridSpec(
            num_scalar_prefetch=1,
            grid=(heads // head_block,),
            in_specs=[
                query_spec,
                slot_spec,
                slot_spec,
                slot_spec,
                slot_spec,
                pl.BlockSpec((head_block, lat_dim, value_dim), lambda i, s: (i, 0, 0)),
            ],
            out_specs=pl.BlockSpec((tokens, head_block * value_dim), lambda i, s: (0, i)),
            scratch_shapes=[
                pltpu.VMEM((context, width), absorbed.dtype),
                pltpu.VMEM((width, context), absorbed.dtype),
                pltpu.VMEM((tokens, context), jnp.float32),
            ],
        ),
        out_shape=jax.ShapeDtypeStruct((tokens, heads * value_dim), absorbed.dtype),
        compiler_params=pltpu.CompilerParams(vmem_limit_bytes=32 << 20),
        cost_estimate=pl.CostEstimate(
            flops=2 * tokens * heads * (context * (width + lat_dim) + lat_dim * value_dim),
            bytes_accessed=2 * (heads * tokens * width + value_up.size + heads * tokens * value_dim),
            transcendentals=heads * tokens * context,
        ),
    )(scalars, absorbed, *slots, value_up)


def project_kernel(
    scalars_ref, own_ref, near_ref, far_ref, cross_ref, weight_ref, keep_ref, send_ref,
    rows_ref, sums_ref,
):
    tokens = own_ref.shape[0]

    @pl.when(pl.program_id(0) == 0)
    def _():
        for slot, ref in enumerate((own_ref, near_ref, far_ref, cross_ref)):
            rows_ref[slot * tokens : (slot + 1) * tokens, :] = ref[...]

    product = jnp.dot(rows_ref[...], weight_ref[...], preferred_element_type=jnp.float32)
    sums_ref[...] = product.reshape(sums_ref.shape)
    parity = scalars_ref[0] % 2
    kept = jnp.where(scalars_ref[0] // 2 == scalars_ref[1], 0, 2)
    for part in range(2):
        offset = parity if part == 0 else 1 - parity
        rows = pl.ds(part * tokens, tokens)
        keep_ref[rows, :] = sums_ref[kept + offset]
        send_ref[rows, :] = sums_ref[2 - kept + offset].astype(send_ref.dtype)


def project(scalars, slots, weight, column_block):
    tokens, depth = slots[0].shape
    columns = weight.shape[1]
    slot_spec = pl.BlockSpec((tokens, depth), lambda i, s: (0, 0))
    half_spec = pl.BlockSpec((2 * tokens, column_block), lambda i, s: (0, i))
    return pl.pallas_call(
        project_kernel,
        grid_spec=pltpu.PrefetchScalarGridSpec(
            num_scalar_prefetch=1,
            grid=(columns // column_block,),
            in_specs=[slot_spec] * 4
            + [pl.BlockSpec((depth, column_block), lambda i, s: (0, i))],
            out_specs=[half_spec, half_spec],
            scratch_shapes=[
                pltpu.VMEM((4 * tokens, depth), weight.dtype),
                pltpu.VMEM((4, tokens, column_block), jnp.float32),
            ],
        ),
        out_shape=[
            jax.ShapeDtypeStruct((2 * tokens, columns), jnp.float32),
            jax.ShapeDtypeStruct((2 * tokens, columns), weight.dtype),
        ],
        compiler_params=pltpu.CompilerParams(vmem_limit_bytes=24 << 20),
        cost_estimate=pl.CostEstimate(
            flops=8 * tokens * depth * columns,
            bytes_accessed=2 * (weight.size + 4 * tokens * depth + 6 * tokens * columns),
            transcendentals=0,
        ),
    )(scalars, *slots, weight)


def gather_slots(value):
    near = exchange(value, "seq", 1)
    far = exchange(value, "seq", 2)
    return [value, near, far, exchange(far, "seq", 1)]


def on_device_pairs(
    q_heads, cache_latent, cache_rope, span_start, prefix_len, key_up, value_up, out_weight
):
    queries = q_heads[0]
    tokens = queries.shape[0]
    head_count, nope_dim, lat_dim = key_up.shape[1:]
    rope_dim = cache_rope.shape[2]
    head_width = nope_dim + rope_dim
    seq_count = lax.axis_size("seq")
    here = lax.axis_index("seq")
    span_len = tokens * seq_count // NSPAN
    span = here * tokens // span_len
    span_first = span_start[0, span]
    scalars = jnp.stack(
        [
            here,
            lax.axis_index("head"),
            span_first,
            prefix_len[0, span],
            span_first + here * tokens % span_len,
        ]
    ).astype(jnp.int32)
    keys = jnp.concatenate([cache_latent[0], cache_rope[0], cache_rope[0]], axis=1)
    key_slots = gather_slots(keys)
    absorbed = absorb(queries, key_up[0], rope_dim, 8)
    chunk = tokens // 4
    parts = []
    for index in range(tokens // chunk):
        head_out = attend(
            scalars, absorbed, key_slots, value_up[0], head_width ** (-0.5),
            index * chunk, chunk, 8,
        )
        parts.append(gather_slots(head_out))
    kept, came = [], []
    for slots in parts:
        keep, send = project(scalars, slots, out_weight[0], 256)
        kept.append(keep)
        came.append(exchange(send, "head", 1))
    rows = []
    for half in range(2):
        for keep, recv in zip(kept, came):
            piece = slice(half * chunk, (half + 1) * chunk)
            rows.append((keep[piece] + recv[piece].astype(jnp.float32)).astype(jnp.bfloat16))
    return jnp.concatenate(rows, axis=0)[None]


def on_device_any(
    q_heads, cache_latent, cache_rope, span_start, prefix_len, key_up, value_up, out_weight
):
    queries_flat = q_heads[0]
    tokens = queries_flat.shape[0]
    head_count = key_up.shape[1]
    nope_dim = key_up.shape[2]
    head_width = queries_flat.shape[1] // head_count
    seq_count = lax.axis_size("seq")
    seq_index = lax.axis_index("seq")
    queries = queries_flat.reshape(tokens, head_count, head_width)
    absorbed = jnp.einsum(
        "thn,hnl->thl", queries[:, :, :nope_dim], key_up[0], preferred_element_type=jnp.float32
    ).astype(jnp.bfloat16)
    rope_query = queries[:, :, nope_dim:]
    softmax_scale = head_width ** (-0.5)
    span_len = tokens * seq_count // NSPAN
    global_row = seq_index * tokens + jnp.arange(tokens, dtype=jnp.int32)
    one_hot = (global_row // span_len)[:, None] == jnp.arange(NSPAN, dtype=jnp.int32)[None, :]
    span_first = jnp.sum(jnp.where(one_hot, span_start[0][None, :], 0), axis=1)
    prefix_row = jnp.sum(jnp.where(one_hot, prefix_len[0][None, :], 0), axis=1)
    token_pos = span_first + global_row % span_len
    latent = lax.all_gather(cache_latent[0], "seq", axis=0, tiled=True)
    rope = lax.all_gather(cache_rope[0], "seq", axis=0, tiled=True)
    key_pos = jnp.arange(latent.shape[0], dtype=jnp.int32)
    visible = (
        (key_pos[None, :] < prefix_row[:, None])
        | (key_pos[None, :] >= span_first[:, None]) & (key_pos[None, :] <= token_pos[:, None])
    )[:, None, :]
    scores = jnp.einsum(
        "thl,kl->thk", absorbed, latent, preferred_element_type=jnp.float32
    ) + jnp.einsum("thr,kr->thk", rope_query, rope, preferred_element_type=jnp.float32)
    scores = jnp.where(visible, scores * softmax_scale, masked_fill)
    peak = jnp.max(scores, axis=2, keepdims=True)
    weights = jnp.where(visible, jnp.exp(scores - peak), 0.0)
    totals = jnp.sum(weights, axis=2)
    summed = jnp.einsum(
        "thk,kl->thl", weights.astype(jnp.bfloat16), latent, preferred_element_type=jnp.float32
    )
    latent_out = (summed / totals[:, :, None]).astype(jnp.bfloat16)
    head_out = (
        jnp.einsum("thl,hlv->thv", latent_out, value_up[0], preferred_element_type=jnp.float32)
        .astype(jnp.bfloat16)
        .reshape(tokens, -1)
    )
    partial_out = jnp.dot(
        lax.all_gather(head_out, "seq", axis=0, tiled=True),
        out_weight[0],
        preferred_element_type=jnp.float32,
    )
    mixed_out = lax.psum_scatter(partial_out, "head", scatter_dimension=0, tiled=True)
    return mixed_out.astype(jnp.bfloat16)[None]


def solution(mesh):
    in_specs = (
        P("section", ("groups", "seq"), "head"),
        P("section", ("groups", "seq"), None),
        P("section", ("groups", "seq"), None),
        P("section", "groups"),
        P("section", "groups"),
        P("section", "head", None, None),
        P("section", "head", None, None),
        P("section", "head", "seq"),
    )
    out_specs = P("section", ("groups", "head"), "seq")
    paired = mesh.shape["seq"] == 4 and mesh.shape["head"] == 2
    return jax.shard_map(
        on_device_pairs if paired else on_device_any,
        mesh=mesh, in_specs=in_specs, out_specs=out_specs, check_vma=False,
    )
```

```python
import functools

import jax
import jax.numpy as jnp
from jax import lax
from jax.experimental import pallas as pl
from jax.experimental.pallas import tpu as pltpu
from jax.sharding import PartitionSpec as P


NSPAN = 2

CHUNKS = 4

masked_fill = -1e30


def exchange(value, axis, distance):
    count = lax.axis_size(axis)
    return lax.ppermute(value, axis, [(i, i ^ distance) for i in range(count)])


def absorb_kernel(query_ref, key_up_ref, out_ref, *, nope_dim, rope_dim):
    heads = key_up_ref.shape[0]
    lat_dim = key_up_ref.shape[2]
    tokens = query_ref.shape[0]
    pair_width = 2 * (nope_dim + rope_dim)
    lane = lax.broadcasted_iota(jnp.int32, (tokens, 2 * rope_dim), 1)
    for pair in range(heads // 2):
        base = pair * pair_width
        even_nope = query_ref[:, base : base + nope_dim]
        even_rope = query_ref[:, base + nope_dim : base + nope_dim + 2 * rope_dim]
        odd_all = query_ref[:, base + nope_dim : base + pair_width]
        odd_rope = query_ref[:, base + pair_width - 2 * rope_dim : base + pair_width]
        pad = jnp.zeros((rope_dim, lat_dim), key_up_ref.dtype)
        odd_map = jnp.concatenate([pad, key_up_ref[2 * pair + 1], pad], axis=0)
        out_ref[2 * pair, :, :lat_dim] = jnp.dot(
            even_nope, key_up_ref[2 * pair], preferred_element_type=jnp.float32
        ).astype(out_ref.dtype)
        out_ref[2 * pair + 1, :, :lat_dim] = jnp.dot(
            odd_all, odd_map, preferred_element_type=jnp.float32
        ).astype(out_ref.dtype)
        zero = jnp.zeros_like(even_rope)
        out_ref[2 * pair, :, lat_dim:] = jnp.where(lane < rope_dim, even_rope, zero)
        out_ref[2 * pair + 1, :, lat_dim:] = jnp.where(lane >= rope_dim, odd_rope, zero)


def absorb(queries, key_up, rope_dim, head_block):
    tokens = queries.shape[0]
    heads, nope_dim, lat_dim = key_up.shape
    head_width = nope_dim + rope_dim
    out_dim = lat_dim + 2 * rope_dim
    return pl.pallas_call(
        functools.partial(absorb_kernel, nope_dim=nope_dim, rope_dim=rope_dim),
        grid=(heads // head_block,),
        in_specs=[
            pl.BlockSpec((tokens, head_block * head_width), lambda i: (0, i)),
            pl.BlockSpec((head_block, nope_dim, lat_dim), lambda i: (i, 0, 0)),
        ],
        out_specs=pl.BlockSpec((head_block, tokens, out_dim), lambda i: (i, 0, 0)),
        out_shape=jax.ShapeDtypeStruct((heads, tokens, out_dim), queries.dtype),
        compiler_params=pltpu.CompilerParams(vmem_limit_bytes=24 << 20),
        cost_estimate=pl.CostEstimate(
            flops=2 * tokens * heads * nope_dim * lat_dim,
            bytes_accessed=2 * (queries.size + key_up.size + heads * tokens * out_dim),
            transcendentals=0,
        ),
    )(queries, key_up)


def attend_kernel(
    start_ref, prefix_ref, query_ref, own_ref, near_ref, far_ref, cross_ref, value_up_ref, out_ref,
    keys_ref, keys_t_ref, hide_ref, *, softmax_scale, lat_dim, first_token,
):
    heads, tokens, width = query_ref.shape
    block = own_ref.shape[0]
    context = keys_ref.shape[0]

    @pl.when(pl.program_id(0) == 0)
    def _():
        for slot, ref in enumerate((own_ref, near_ref, far_ref, cross_ref)):
            keys_ref[slot * block : (slot + 1) * block, :] = ref[...]
        keys_t_ref[...] = keys_ref[...].T
        here = lax.axis_index("seq")
        span_blocks = context // block // NSPAN
        span_first = start_ref[here // span_blocks]
        prefix = prefix_ref[here // span_blocks]
        first_pos = span_first + here % span_blocks * block + first_token
        column = lax.broadcasted_iota(jnp.int32, (tokens, context), 1)
        row = lax.broadcasted_iota(jnp.int32, (tokens, context), 0)
        position = lax.bitwise_xor(column // block, here) * block + column % block
        visible = (position < prefix) | (
            (position >= span_first) & (position <= row + first_pos)
        )
        hide_ref[...] = jnp.where(visible, 0.0, masked_fill)

    query = query_ref[...].reshape(heads * tokens, width)
    scores = jnp.dot(query, keys_t_ref[...], preferred_element_type=jnp.float32)
    scores = scores.reshape(heads, tokens, context) + hide_ref[...][None]
    peak = jnp.max(scores, axis=2, keepdims=True)
    weights = jnp.exp((scores - peak) * softmax_scale)
    inverse = 1.0 / jnp.sum(weights, axis=2, keepdims=True)
    rounded = weights.astype(keys_ref.dtype).reshape(heads * tokens, context)
    summed = jnp.dot(rounded, keys_ref[:, :lat_dim], preferred_element_type=jnp.float32)
    latent_out = (summed.reshape(heads, tokens, lat_dim) * inverse).astype(keys_ref.dtype)
    value_dim = value_up_ref.shape[2]
    for head in range(heads):
        out_ref[:, head * value_dim : (head + 1) * value_dim] = jnp.dot(
            latent_out[head], value_up_ref[head], preferred_element_type=jnp.float32
        ).astype(out_ref.dtype)


def attend(spans, absorbed, slots, value_up, softmax_scale, first_token, tokens, head_block):
    heads, _, width = absorbed.shape
    _, lat_dim, value_dim = value_up.shape
    block = slots[0].shape[0]
    context = block * len(slots)
    step = first_token // tokens if first_token % tokens == 0 else None
    slot_spec = pl.BlockSpec((block, width), lambda i, *_: (0, 0))
    query_spec = pl.BlockSpec(
        (head_block, pl.Element(tokens), width), lambda i, *_: (i, first_token, 0)
    )
    if step is not None:
        query_spec = pl.BlockSpec((head_block, tokens, width), lambda i, *_: (i, step, 0))
    return pl.pallas_call(
        functools.partial(
            attend_kernel, softmax_scale=softmax_scale, lat_dim=lat_dim,
            first_token=first_token,
        ),
        grid_spec=pltpu.PrefetchScalarGridSpec(
            num_scalar_prefetch=2,
            grid=(heads // head_block,),
            in_specs=[
                query_spec,
                slot_spec,
                slot_spec,
                slot_spec,
                slot_spec,
                pl.BlockSpec((head_block, lat_dim, value_dim), lambda i, *_: (i, 0, 0)),
            ],
            out_specs=pl.BlockSpec((tokens, head_block * value_dim), lambda i, *_: (0, i)),
            scratch_shapes=[
                pltpu.VMEM((context, width), absorbed.dtype),
                pltpu.VMEM((width, context), absorbed.dtype),
                pltpu.VMEM((tokens, context), jnp.float32),
            ],
        ),
        out_shape=jax.ShapeDtypeStruct((tokens, heads * value_dim), absorbed.dtype),
        compiler_params=pltpu.CompilerParams(vmem_limit_bytes=32 << 20),
        cost_estimate=pl.CostEstimate(
            flops=2 * tokens * heads * (context * (width + lat_dim) + lat_dim * value_dim),
            bytes_accessed=2 * (heads * tokens * width + value_up.size + heads * tokens * value_dim),
            transcendentals=heads * tokens * context,
        ),
    )(*spans, absorbed, *slots, value_up)


def project_kernel(
    own_ref, near_ref, far_ref, cross_ref, weight_ref, keep_ref, send_ref,
    rows_ref, sums_ref,
):
    tokens = own_ref.shape[0]

    @pl.when(pl.program_id(0) == 0)
    def _():
        for slot, ref in enumerate((own_ref, near_ref, far_ref, cross_ref)):
            rows_ref[slot * tokens : (slot + 1) * tokens, :] = ref[...]

    product = jnp.dot(rows_ref[...], weight_ref[...], preferred_element_type=jnp.float32)
    sums_ref[...] = product.reshape(sums_ref.shape)
    here = lax.axis_index("seq")
    parity = here % 2
    kept = jnp.where(here // 2 == lax.axis_index("head"), 0, 2)
    for part in range(2):
        offset = parity if part == 0 else 1 - parity
        rows = pl.ds(part * tokens, tokens)
        keep_ref[rows, :] = sums_ref[kept + offset]
        send_ref[rows, :] = sums_ref[2 - kept + offset].astype(send_ref.dtype)


def project(slots, weight, column_block):
    tokens, depth = slots[0].shape
    columns = weight.shape[1]
    slot_spec = pl.BlockSpec((tokens, depth), lambda i, *_: (0, 0))
    half_spec = pl.BlockSpec((2 * tokens, column_block), lambda i, *_: (0, i))
    return pl.pallas_call(
        project_kernel,
        grid_spec=pltpu.PrefetchScalarGridSpec(
            num_scalar_prefetch=0,
            grid=(columns // column_block,),
            in_specs=[slot_spec] * 4
            + [pl.BlockSpec((depth, column_block), lambda i, *_: (0, i))],
            out_specs=[half_spec, half_spec],
            scratch_shapes=[
                pltpu.VMEM((4 * tokens, depth), weight.dtype),
                pltpu.VMEM((4, tokens, column_block), jnp.float32),
            ],
        ),
        out_shape=[
            jax.ShapeDtypeStruct((2 * tokens, columns), jnp.float32),
            jax.ShapeDtypeStruct((2 * tokens, columns), weight.dtype),
        ],
        compiler_params=pltpu.CompilerParams(vmem_limit_bytes=24 << 20),
        cost_estimate=pl.CostEstimate(
            flops=8 * tokens * depth * columns,
            bytes_accessed=2 * (weight.size + 4 * tokens * depth + 6 * tokens * columns),
            transcendentals=0,
        ),
    )(*slots, weight)


def on_device_pairs(
    q_heads, cache_latent, cache_rope, span_start, prefix_len, key_up, value_up, out_weight
):
    queries = q_heads[0]
    tokens = queries.shape[0]
    nope_dim = key_up.shape[2]
    rope_dim = cache_rope.shape[2]
    spans = (span_start[0], prefix_len[0])
    keys = jnp.concatenate([cache_latent[0], cache_rope[0], cache_rope[0]], axis=1)
    far = exchange(keys, "seq", 2)
    near = exchange(keys, "seq", 1)
    absorbed = absorb(queries, key_up[0], rope_dim, 8)
    cross = exchange(far, "seq", 1)
    key_slots = [keys, near, far, cross]
    chunk = tokens // CHUNKS
    parts = []
    for index in range(CHUNKS):
        own = attend(
            spans, absorbed, key_slots, value_up[0], (nope_dim + rope_dim) ** (-0.5),
            index * chunk, chunk, 8,
        )
        far = exchange(own, "seq", 2)
        near = exchange(own, "seq", 1)
        cross = exchange(far, "seq", 1)
        parts.append([own, near, far, cross])
    kept, came = [], []
    for slots in parts:
        keep, send = project(slots, out_weight[0], 256)
        kept.append(keep)
        came.append(exchange(send, "head", 1))
    rows = []
    for half in range(2):
        for keep, recv in zip(kept, came):
            piece = slice(half * chunk, (half + 1) * chunk)
            rows.append((keep[piece] + recv[piece].astype(jnp.float32)).astype(jnp.bfloat16))
    return jnp.concatenate(rows, axis=0)[None]


def on_device_any(
    q_heads, cache_latent, cache_rope, span_start, prefix_len, key_up, value_up, out_weight
):
    queries_flat = q_heads[0]
    tokens = queries_flat.shape[0]
    head_count = key_up.shape[1]
    nope_dim = key_up.shape[2]
    head_width = queries_flat.shape[1] // head_count
    seq_count = lax.axis_size("seq")
    seq_index = lax.axis_index("seq")
    queries = queries_flat.reshape(tokens, head_count, head_width)
    absorbed = jnp.einsum(
        "thn,hnl->thl", queries[:, :, :nope_dim], key_up[0], preferred_element_type=jnp.float32
    ).astype(jnp.bfloat16)
    rope_query = queries[:, :, nope_dim:]
    softmax_scale = head_width ** (-0.5)
    span_len = tokens * seq_count // NSPAN
    global_row = seq_index * tokens + jnp.arange(tokens, dtype=jnp.int32)
    one_hot = (global_row // span_len)[:, None] == jnp.arange(NSPAN, dtype=jnp.int32)[None, :]
    span_first = jnp.sum(jnp.where(one_hot, span_start[0][None, :], 0), axis=1)
    prefix_row = jnp.sum(jnp.where(one_hot, prefix_len[0][None, :], 0), axis=1)
    token_pos = span_first + global_row % span_len
    latent = lax.all_gather(cache_latent[0], "seq", axis=0, tiled=True)
    rope = lax.all_gather(cache_rope[0], "seq", axis=0, tiled=True)
    key_pos = jnp.arange(latent.shape[0], dtype=jnp.int32)
    visible = (
        (key_pos[None, :] < prefix_row[:, None])
        | (key_pos[None, :] >= span_first[:, None]) & (key_pos[None, :] <= token_pos[:, None])
    )[:, None, :]
    scores = jnp.einsum(
        "thl,kl->thk", absorbed, latent, preferred_element_type=jnp.float32
    ) + jnp.einsum("thr,kr->thk", rope_query, rope, preferred_element_type=jnp.float32)
    scores = jnp.where(visible, scores * softmax_scale, masked_fill)
    peak = jnp.max(scores, axis=2, keepdims=True)
    weights = jnp.where(visible, jnp.exp(scores - peak), 0.0)
    totals = jnp.sum(weights, axis=2)
    summed = jnp.einsum(
        "thk,kl->thl", weights.astype(jnp.bfloat16), latent, preferred_element_type=jnp.float32
    )
    latent_out = (summed / totals[:, :, None]).astype(jnp.bfloat16)
    head_out = (
        jnp.einsum("thl,hlv->thv", latent_out, value_up[0], preferred_element_type=jnp.float32)
        .astype(jnp.bfloat16)
        .reshape(tokens, -1)
    )
    partial_out = jnp.dot(
        lax.all_gather(head_out, "seq", axis=0, tiled=True),
        out_weight[0],
        preferred_element_type=jnp.float32,
    )
    mixed_out = lax.psum_scatter(partial_out, "head", scatter_dimension=0, tiled=True)
    return mixed_out.astype(jnp.bfloat16)[None]


def solution(mesh):
    in_specs = (
        P("section", ("groups", "seq"), "head"),
        P("section", ("groups", "seq"), None),
        P("section", ("groups", "seq"), None),
        P("section", "groups"),
        P("section", "groups"),
        P("section", "head", None, None),
        P("section", "head", None, None),
        P("section", "head", "seq"),
    )
    out_specs = P("section", ("groups", "head"), "seq")
    paired = mesh.shape["seq"] == 4 and mesh.shape["head"] == 2
    return jax.shard_map(
        on_device_pairs if paired else on_device_any,
        mesh=mesh, in_specs=in_specs, out_specs=out_specs, check_vma=False,
    )
```

```python
import functools

import jax
import jax.numpy as jnp
from jax import lax
from jax.experimental import pallas as pl
from jax.experimental.pallas import tpu as pltpu
from jax.sharding import PartitionSpec as P


NSPAN = 2

SHARES = (2, 2, 2, 2)
CHUNKS = len(SHARES)
PREPARE_FLOPS = 10_000_000_000
EVERYWHERE_SHARE = 8
DIRECT = (False, False, False, False)

masked_fill = -1e30

VMEM = pl.BlockSpec(memory_space=pltpu.VMEM)
SMEM = pl.BlockSpec(memory_space=pltpu.SMEM)


def exchange(value, axis, distance):
    count = lax.axis_size(axis)
    return lax.ppermute(value, axis, [(i, i ^ distance) for i in range(count)])


def prepare_kernel(latent_ref, rope_ref, keys_ref, half_ref, loaded_ref, sems):
    lat_dim = latent_ref.shape[1]
    half = half_ref.shape[0]
    latent_copy = pltpu.make_async_copy(latent_ref, keys_ref.at[:, :lat_dim], sems.at[0])
    rope_copy = pltpu.make_async_copy(rope_ref, loaded_ref, sems.at[1])
    latent_copy.start()
    rope_copy.start()
    rope_copy.wait()
    keys_ref[:, lat_dim:] = jnp.concatenate([loaded_ref[...]] * 2, axis=0).T
    latent_copy.wait()
    first = pl.multiple_of(lax.axis_index("head") * half, half)
    half_ref[...] = keys_ref[pl.ds(first, half), :]


def prepare(latent, rope):
    tokens, lat_dim = latent.shape
    rope_dim = rope.shape[0]
    width = lat_dim + 2 * rope_dim
    return pl.pallas_call(
        prepare_kernel,
        in_specs=[pl.BlockSpec(memory_space=pl.ANY)] * 2,
        out_specs=[VMEM] * 2,
        scratch_shapes=[
            pltpu.VMEM((rope_dim, tokens), rope.dtype),
            pltpu.SemaphoreType.DMA((2,)),
        ],
        out_shape=[
            jax.ShapeDtypeStruct((tokens, width), latent.dtype),
            jax.ShapeDtypeStruct((tokens // 2, width), latent.dtype),
        ],
        compiler_params=pltpu.CompilerParams(vmem_limit_bytes=2 << 20),
        cost_estimate=pl.CostEstimate(
            flops=PREPARE_FLOPS, bytes_accessed=4 * latent.size, transcendentals=0
        ),
    )(latent, rope)


def absorb_into(query_ref, key_up_ref, out_ref, first_head, nope_dim, rope_dim):
    heads, tokens, _ = out_ref.shape
    lat_dim = key_up_ref.shape[2]
    pair_width = 2 * (nope_dim + rope_dim)
    lane = lax.broadcasted_iota(jnp.int32, (tokens, 2 * rope_dim), 1)
    pad = jnp.zeros((rope_dim, lat_dim), key_up_ref.dtype)
    for head in range(0, heads, 2):
        base = head // 2 * pair_width
        even_nope = query_ref[:, base : base + nope_dim]
        even_rope = query_ref[:, base + nope_dim : base + nope_dim + 2 * rope_dim]
        odd_all = query_ref[:, base + nope_dim : base + pair_width]
        odd_rope = query_ref[:, base + pair_width - 2 * rope_dim : base + pair_width]
        odd_map = jnp.concatenate([pad, key_up_ref[first_head + head + 1], pad], axis=0)
        out_ref[head, :, :lat_dim] = jnp.dot(
            even_nope, key_up_ref[first_head + head], preferred_element_type=jnp.float32
        ).astype(out_ref.dtype)
        out_ref[head + 1, :, :lat_dim] = jnp.dot(
            odd_all, odd_map, preferred_element_type=jnp.float32
        ).astype(out_ref.dtype)
        zero = jnp.zeros_like(even_rope)
        out_ref[head, :, lat_dim:] = jnp.where(lane < rope_dim, even_rope, zero)
        out_ref[head + 1, :, lat_dim:] = jnp.where(lane >= rope_dim, odd_rope, zero)


def absorb(queries, key_up, rope_dim, heads):
    tokens = queries.shape[0]
    _, nope_dim, lat_dim = key_up.shape
    out_dim = lat_dim + 2 * rope_dim

    def kernel(query_ref, key_up_ref, out_ref):
        absorb_into(query_ref, key_up_ref, out_ref, 0, nope_dim, rope_dim)

    return pl.pallas_call(
        kernel,
        in_specs=[VMEM] * 2,
        out_specs=VMEM,
        out_shape=jax.ShapeDtypeStruct((heads, tokens, out_dim), queries.dtype),
        compiler_params=pltpu.CompilerParams(vmem_limit_bytes=12 << 20),
        cost_estimate=pl.CostEstimate(
            flops=2 * tokens * heads * nope_dim * lat_dim,
            bytes_accessed=2 * (queries.size + key_up.size + heads * tokens * out_dim),
            transcendentals=0,
        ),
    )(queries, key_up)


def load_keys(own_ref, mine_refs, other_refs, keys_ref, keys_t_ref):
    block = own_ref.shape[0]
    half = block // 2
    keys_ref[:block, :] = own_ref[...]
    mine = lax.axis_index("head") * half
    for slot in range(1, 4):
        first = pl.multiple_of(slot * block + mine, half)
        keys_ref[pl.ds(first, half), :] = mine_refs[slot - 1][...]
        first = pl.multiple_of(slot * block + half - mine, half)
        keys_ref[pl.ds(first, half), :] = other_refs[slot - 1][...]
    keys_t_ref[...] = keys_ref[...].T


def hide_of(start_ref, prefix_ref, slot, first_token, tokens, block, context):
    here = lax.axis_index("seq")
    there = lax.bitwise_xor(here, slot)
    span_blocks = context // block // NSPAN
    span_first = start_ref[there // span_blocks]
    prefix = prefix_ref[there // span_blocks]
    first_pos = span_first + there % span_blocks * block + first_token
    column = lax.broadcasted_iota(jnp.int32, (tokens, context), 1)
    row = lax.broadcasted_iota(jnp.int32, (tokens, context), 0)
    position = lax.bitwise_xor(column // block, here) * block + column % block
    visible = (position < prefix) | ((position >= span_first) & (position <= row + first_pos))
    return jnp.where(visible, 0.0, masked_fill)


def attention(query, keys_ref, keys_t_ref, hide, softmax_scale, lat_dim):
    heads, tokens, width = query.shape
    context = keys_ref.shape[0]
    scores = jnp.dot(
        query.reshape(heads * tokens, width), keys_t_ref[...], preferred_element_type=jnp.float32
    )
    scores = scores.reshape(heads, tokens, context) + hide[None]
    peak = jnp.max(scores, axis=2, keepdims=True)
    weights = jnp.exp((scores - peak) * softmax_scale)
    inverse = 1.0 / jnp.sum(weights, axis=2, keepdims=True)
    rounded = weights.astype(keys_ref.dtype).reshape(heads * tokens, context)
    summed = jnp.dot(rounded, keys_ref[:, :lat_dim], preferred_element_type=jnp.float32)
    return (summed.reshape(heads, tokens, lat_dim) * inverse).astype(keys_ref.dtype)


def attend_heads(
    start_ref, prefix_ref, query_ref, value_up_ref, keys_ref, keys_t_ref, out_ref,
    softmax_scale, first_token, head_block,
):
    heads, block, _ = query_ref.shape
    tokens = out_ref.shape[0]
    _, lat_dim, value_dim = value_up_ref.shape
    hide = hide_of(start_ref, prefix_ref, 0, first_token, tokens, block, keys_ref.shape[0])
    for base in range(0, heads, head_block):
        latent_out = attention(
            query_ref[base : base + head_block, first_token : first_token + tokens, :],
            keys_ref, keys_t_ref, hide, softmax_scale, lat_dim,
        )
        for head in range(head_block):
            out_ref[:, (base + head) * value_dim : (base + head + 1) * value_dim] = jnp.dot(
                latent_out[head], value_up_ref[base + head], preferred_element_type=jnp.float32
            ).astype(out_ref.dtype)


def attend_kernel(
    start_ref, prefix_ref, query_ref, value_up_ref, *refs, softmax_scale, first_token, head_block
):
    if len(refs) > 3:
        own_ref, *received, out_ref, keys_ref, keys_t_ref = refs
        load_keys(own_ref, received[:3], received[3:], keys_ref, keys_t_ref)
    else:
        keys_ref, keys_t_ref, out_ref = refs
    attend_heads(
        start_ref, prefix_ref, query_ref, value_up_ref, keys_ref, keys_t_ref, out_ref,
        softmax_scale, first_token, head_block,
    )


def attend(spans, absorbed, keys, value_up, softmax_scale, first_token, tokens, context):
    heads, _, width = absorbed.shape
    _, lat_dim, value_dim = value_up.shape
    out_shape = [jax.ShapeDtypeStruct((tokens, heads * value_dim), absorbed.dtype)]
    if len(keys) > 2:
        out_shape.append(jax.ShapeDtypeStruct((context, width), absorbed.dtype))
        out_shape.append(jax.ShapeDtypeStruct((width, context), absorbed.dtype))
    return pl.pallas_call(
        functools.partial(
            attend_kernel,
            softmax_scale=softmax_scale,
            first_token=first_token,
            head_block=heads // 2,
        ),
        in_specs=[SMEM] * 2 + [VMEM] * (2 + len(keys)),
        out_specs=[VMEM] * len(out_shape),
        out_shape=out_shape,
        compiler_params=pltpu.CompilerParams(vmem_limit_bytes=24 << 20),
        cost_estimate=pl.CostEstimate(
            flops=2 * tokens * heads * (context * (width + lat_dim) + lat_dim * value_dim),
            bytes_accessed=2 * (heads * tokens * width + value_up.size + heads * tokens * value_dim),
            transcendentals=heads * tokens * context,
        ),
    )(*spans, absorbed, value_up, *keys)


def everywhere_kernel(
    start_ref, prefix_ref, query0_ref, query1_ref, query2_ref, query3_ref,
    keys_ref, keys_t_ref, key_up_ref, value_up_ref, out_ref,
    queries_ref, absorbed_ref, *, softmax_scale, rope_dim, first_head,
):
    tokens = query0_ref.shape[0]
    _, nope_dim, lat_dim = key_up_ref.shape
    value_dim = value_up_ref.shape[2]
    heads = absorbed_ref.shape[0]
    for slot, ref in enumerate((query0_ref, query1_ref, query2_ref, query3_ref)):
        queries_ref[slot * tokens : (slot + 1) * tokens, :] = ref[...]
    absorb_into(queries_ref, key_up_ref, absorbed_ref, first_head, nope_dim, rope_dim)
    for slot in range(4):
        rows = slice(slot * tokens, (slot + 1) * tokens)
        latent_out = attention(
            absorbed_ref[:, rows, :], keys_ref, keys_t_ref,
            hide_of(start_ref, prefix_ref, slot, 0, tokens, tokens, keys_ref.shape[0]),
            softmax_scale, lat_dim,
        )
        for head in range(heads):
            out_ref[rows, head * value_dim : (head + 1) * value_dim] = jnp.dot(
                latent_out[head], value_up_ref[first_head + head],
                preferred_element_type=jnp.float32,
            ).astype(out_ref.dtype)


def attend_everywhere(spans, query_slots, keys, key_up, value_up, softmax_scale, rope_dim):
    tokens, width = query_slots[0].shape
    heads = width // (key_up.shape[1] + rope_dim)
    _, lat_dim, value_dim = value_up.shape
    context, key_width = keys[0].shape
    return pl.pallas_call(
        functools.partial(
            everywhere_kernel,
            softmax_scale=softmax_scale,
            rope_dim=rope_dim,
            first_head=key_up.shape[0] - heads,
        ),
        in_specs=[SMEM] * 2 + [VMEM] * 8,
        out_specs=VMEM,
        scratch_shapes=[
            pltpu.VMEM((4 * tokens, width), key_up.dtype),
            pltpu.VMEM((heads, 4 * tokens, key_width), key_up.dtype),
        ],
        out_shape=jax.ShapeDtypeStruct((4 * tokens, heads * value_dim), key_up.dtype),
        compiler_params=pltpu.CompilerParams(vmem_limit_bytes=24 << 20),
        cost_estimate=pl.CostEstimate(
            flops=8 * tokens * heads * (context * (key_width + lat_dim) + 2 * lat_dim * value_dim),
            bytes_accessed=8 * tokens * (width + heads * value_dim),
            transcendentals=4 * heads * tokens * context,
        ),
    )(*spans, *query_slots, *keys, key_up, value_up)


def project_kernel(
    own_ref, near_ref, far_ref, cross_ref, everywhere_ref, weight_ref, keep_ref, send_ref,
    rows_ref, sums_ref, *, first_token, first_column,
):
    tokens, split = own_ref.shape
    block = everywhere_ref.shape[0] // 4
    columns = keep_ref.shape[1]
    column_block = sums_ref.shape[2]
    for slot, ref in enumerate((own_ref, near_ref, far_ref, cross_ref)):
        rows = slice(slot * tokens, (slot + 1) * tokens)
        first = slot * block + first_token
        rows_ref[rows, :split] = ref[...]
        rows_ref[rows, split:] = everywhere_ref[first : first + tokens, :]
    here = lax.axis_index("seq")
    parity = here % 2
    kept = jnp.where(here // 2 == lax.axis_index("head"), 0, 2)
    for base in range(0, columns, column_block):
        product = jnp.dot(
            rows_ref[...],
            weight_ref[:, first_column + base : first_column + base + column_block],
            preferred_element_type=jnp.float32,
        )
        sums_ref[...] = product.reshape(sums_ref.shape)
        for part in range(2):
            offset = parity if part == 0 else 1 - parity
            rows = slice(part * tokens, (part + 1) * tokens)
            target = slice(base, base + column_block)
            keep_ref[rows, target] = sums_ref[kept + offset]
            send_ref[rows, target] = sums_ref[2 - kept + offset].astype(send_ref.dtype)


def project(slots, everywhere, weight, first_token, first_column, columns, column_block):
    tokens = slots[0].shape[0]
    depth = weight.shape[0]
    return pl.pallas_call(
        functools.partial(project_kernel, first_token=first_token, first_column=first_column),
        in_specs=[VMEM] * 6,
        out_specs=[VMEM] * 2,
        scratch_shapes=[
            pltpu.VMEM((4 * tokens, depth), weight.dtype),
            pltpu.VMEM((4, tokens, column_block), jnp.float32),
        ],
        out_shape=[
            jax.ShapeDtypeStruct((2 * tokens, columns), jnp.float32),
            jax.ShapeDtypeStruct((2 * tokens, columns), weight.dtype),
        ],
        compiler_params=pltpu.CompilerParams(vmem_limit_bytes=12 << 20),
        cost_estimate=pl.CostEstimate(
            flops=8 * tokens * depth * columns,
            bytes_accessed=2 * (depth * columns + 4 * tokens * depth + 6 * tokens * columns),
            transcendentals=0,
        ),
    )(*slots, everywhere, weight)


def finish_kernel(*refs, firsts, aliased):
    count = len(firsts)
    out_ref, sums_ref, sems = refs[-3:]
    refs = refs[aliased : aliased + 2 * count]
    half = out_ref.shape[0] // 2
    copies = []
    done = 0
    for index, first in enumerate(firsts):
        keep_ref, came_ref = refs[index], refs[count + index]
        tokens = keep_ref.shape[0] // 2
        sums_ref[done : done + 2 * tokens, :] = (
            keep_ref[...] + came_ref[...].astype(jnp.float32)
        ).astype(sums_ref.dtype)
        for part in range(2):
            copies.append(
                pltpu.make_async_copy(
                    sums_ref.at[pl.ds(done + part * tokens, tokens), :],
                    out_ref.at[pl.ds(part * half + first, tokens), :],
                    sems.at[2 * index + part],
                )
            )
            copies[-1].start()
        done += 2 * tokens
    for copy in copies:
        copy.wait()


def finish(partial, kept, came, firsts, rows):
    columns = kept[0].shape[1]
    before = [] if partial is None else [partial]
    return pl.pallas_call(
        functools.partial(finish_kernel, firsts=firsts, aliased=len(before)),
        in_specs=[pl.BlockSpec(memory_space=pl.ANY)] * len(before) + [VMEM] * (2 * len(kept)),
        out_specs=pl.BlockSpec(memory_space=pl.ANY),
        scratch_shapes=[
            pltpu.VMEM((sum(keep.shape[0] for keep in kept), columns), came[0].dtype),
            pltpu.SemaphoreType.DMA((2 * len(kept),)),
        ],
        out_shape=jax.ShapeDtypeStruct((rows, columns), came[0].dtype),
        input_output_aliases={0: 0} if before else {},
        compiler_params=pltpu.CompilerParams(vmem_limit_bytes=4 << 20),
        cost_estimate=pl.CostEstimate(
            flops=sum(keep.size for keep in kept),
            bytes_accessed=8 * sum(keep.size for keep in kept),
            transcendentals=0,
        ),
    )(*before, *kept, *came)


def on_device_pairs(
    q_heads, cache_latent, cache_rope, span_start, prefix_len, key_up, value_up, out_weight
):
    queries = q_heads[0]
    tokens = queries.shape[0]
    head_count, nope_dim = key_up.shape[1:3]
    rope_dim = cache_rope.shape[2]
    head_width = nope_dim + rope_dim
    softmax_scale = head_width ** (-0.5)
    columns = out_weight.shape[2]
    everywhere_heads = head_count // EVERYWHERE_SHARE
    sent_heads = head_count - everywhere_heads
    context = tokens * lax.axis_size("seq")
    spans = (span_start[0], prefix_len[0])
    sizes = [tokens * share // sum(SHARES) for share in SHARES]
    firsts = [sum(sizes[:index]) for index in range(CHUNKS)]
    own, half = prepare(cache_latent[0], cache_rope[0].T)
    far = exchange(half, "seq", 2)
    near = exchange(half, "seq", 1)
    absorbed = absorb(queries, key_up[0], rope_dim, sent_heads)
    cross = exchange(far, "seq", 1)
    near_x = exchange(near, "head", 1)
    far_x = exchange(far, "head", 1)
    cross_x = exchange(cross, "head", 1)
    keys = [own, near, far, cross, near_x, far_x, cross_x]
    own = queries[:, sent_heads * head_width :]
    far = exchange(own, "seq", 2)
    near = exchange(own, "seq", 1)
    cross = exchange(far, "seq", 1)
    query_slots = [own, near, far, cross]
    parts = []
    for index in range(CHUNKS):
        own, *rest = attend(
            spans, absorbed, keys, value_up[0], softmax_scale, firsts[index],
            sizes[index], context,
        )
        keys = rest or keys
        far = exchange(own, "seq", 2)
        near = exchange(own, "seq", 1)
        if DIRECT[index]:
            cross = exchange(own, "seq", 3)
        else:
            cross = exchange(far, "seq", 1)
        parts.append([own, near, far, cross])
    everywhere = attend_everywhere(
        spans, query_slots, keys, key_up[0], value_up[0], softmax_scale, rope_dim
    )
    kept, came = [], []
    for index, slots in enumerate(parts):
        keep, sent = project(
            slots, everywhere, out_weight[0], firsts[index], 0, columns, columns // 2
        )
        kept.append(keep)
        came.append(exchange(sent, "head", 1))
    out = finish(None, kept[:-1], came[:-1], firsts[:-1], 2 * tokens)
    out = finish(out, kept[-1:], came[-1:], firsts[-1:], 2 * tokens)
    return out[None]


def on_device_any(
    q_heads, cache_latent, cache_rope, span_start, prefix_len, key_up, value_up, out_weight
):
    queries_flat = q_heads[0]
    tokens = queries_flat.shape[0]
    head_count = key_up.shape[1]
    nope_dim = key_up.shape[2]
    head_width = queries_flat.shape[1] // head_count
    seq_count = lax.axis_size("seq")
    seq_index = lax.axis_index("seq")
    queries = queries_flat.reshape(tokens, head_count, head_width)
    absorbed = jnp.einsum(
        "thn,hnl->thl", queries[:, :, :nope_dim], key_up[0], preferred_element_type=jnp.float32
    ).astype(jnp.bfloat16)
    rope_query = queries[:, :, nope_dim:]
    softmax_scale = head_width ** (-0.5)
    span_len = tokens * seq_count // NSPAN
    global_row = seq_index * tokens + jnp.arange(tokens, dtype=jnp.int32)
    one_hot = (global_row // span_len)[:, None] == jnp.arange(NSPAN, dtype=jnp.int32)[None, :]
    span_first = jnp.sum(jnp.where(one_hot, span_start[0][None, :], 0), axis=1)
    prefix_row = jnp.sum(jnp.where(one_hot, prefix_len[0][None, :], 0), axis=1)
    token_pos = span_first + global_row % span_len
    latent = lax.all_gather(cache_latent[0], "seq", axis=0, tiled=True)
    rope = lax.all_gather(cache_rope[0], "seq", axis=0, tiled=True)
    key_pos = jnp.arange(latent.shape[0], dtype=jnp.int32)
    visible = (
        (key_pos[None, :] < prefix_row[:, None])
        | (key_pos[None, :] >= span_first[:, None]) & (key_pos[None, :] <= token_pos[:, None])
    )[:, None, :]
    scores = jnp.einsum(
        "thl,kl->thk", absorbed, latent, preferred_element_type=jnp.float32
    ) + jnp.einsum("thr,kr->thk", rope_query, rope, preferred_element_type=jnp.float32)
    scores = jnp.where(visible, scores * softmax_scale, masked_fill)
    peak = jnp.max(scores, axis=2, keepdims=True)
    weights = jnp.where(visible, jnp.exp(scores - peak), 0.0)
    totals = jnp.sum(weights, axis=2)
    summed = jnp.einsum(
        "thk,kl->thl", weights.astype(jnp.bfloat16), latent, preferred_element_type=jnp.float32
    )
    latent_out = (summed / totals[:, :, None]).astype(jnp.bfloat16)
    head_out = (
        jnp.einsum("thl,hlv->thv", latent_out, value_up[0], preferred_element_type=jnp.float32)
        .astype(jnp.bfloat16)
        .reshape(tokens, -1)
    )
    partial_out = jnp.dot(
        lax.all_gather(head_out, "seq", axis=0, tiled=True),
        out_weight[0],
        preferred_element_type=jnp.float32,
    )
    mixed_out = lax.psum_scatter(partial_out, "head", scatter_dimension=0, tiled=True)
    return mixed_out.astype(jnp.bfloat16)[None]


def solution(mesh):
    in_specs = (
        P("section", ("groups", "seq"), "head"),
        P("section", ("groups", "seq"), None),
        P("section", ("groups", "seq"), None),
        P("section", "groups"),
        P("section", "groups"),
        P("section", "head", None, None),
        P("section", "head", None, None),
        P("section", "head", "seq"),
    )
    out_specs = P("section", ("groups", "head"), "seq")
    paired = mesh.shape["seq"] == 4 and mesh.shape["head"] == 2
    return jax.shard_map(
        on_device_pairs if paired else on_device_any,
        mesh=mesh, in_specs=in_specs, out_specs=out_specs, check_vma=False,
    )
```

```python
import functools

import jax
import jax.numpy as jnp
from jax import lax
from jax.experimental import pallas as pl
from jax.experimental.pallas import tpu as pltpu
from jax.sharding import PartitionSpec as P


NSPAN = 2

SHARES = (2, 2, 2, 2)
CHUNKS = len(SHARES)
PREPARE_FLOPS = 10_000_000_000
EVERYWHERE_SHARE = 8
DIRECT = (False, False, False, False)

masked_fill = -1e30

VMEM = pl.BlockSpec(memory_space=pltpu.VMEM)
SMEM = pl.BlockSpec(memory_space=pltpu.SMEM)


def exchange(value, axis, distance):
    count = lax.axis_size(axis)
    return lax.ppermute(value, axis, [(i, i ^ distance) for i in range(count)])


def prepare_kernel(latent_ref, rope_ref, keys_ref, half_ref, loaded_ref, sems):
    lat_dim = latent_ref.shape[1]
    half = half_ref.shape[0]
    latent_copy = pltpu.make_async_copy(latent_ref, keys_ref.at[:, :lat_dim], sems.at[0])
    rope_copy = pltpu.make_async_copy(rope_ref, loaded_ref, sems.at[1])
    latent_copy.start()
    rope_copy.start()
    rope_copy.wait()
    keys_ref[:, lat_dim:] = jnp.concatenate([loaded_ref[...]] * 2, axis=0).T
    latent_copy.wait()
    first = pl.multiple_of(lax.axis_index("head") * half, half)
    half_ref[...] = keys_ref[pl.ds(first, half), :]


def prepare(latent, rope):
    tokens, lat_dim = latent.shape
    rope_dim = rope.shape[0]
    width = lat_dim + 2 * rope_dim
    return pl.pallas_call(
        prepare_kernel,
        in_specs=[pl.BlockSpec(memory_space=pl.ANY)] * 2,
        out_specs=[VMEM] * 2,
        scratch_shapes=[
            pltpu.VMEM((rope_dim, tokens), rope.dtype),
            pltpu.SemaphoreType.DMA((2,)),
        ],
        out_shape=[
            jax.ShapeDtypeStruct((tokens, width), latent.dtype),
            jax.ShapeDtypeStruct((tokens // 2, width), latent.dtype),
        ],
        compiler_params=pltpu.CompilerParams(vmem_limit_bytes=2 << 20),
        cost_estimate=pl.CostEstimate(
            flops=PREPARE_FLOPS, bytes_accessed=4 * latent.size, transcendentals=0
        ),
    )(latent, rope)


def absorb_into(query_ref, key_up_ref, out_ref, first_head, nope_dim, rope_dim):
    heads, tokens, _ = out_ref.shape
    lat_dim = key_up_ref.shape[2]
    pair_width = 2 * (nope_dim + rope_dim)
    lane = lax.broadcasted_iota(jnp.int32, (tokens, 2 * rope_dim), 1)
    pad = jnp.zeros((rope_dim, lat_dim), key_up_ref.dtype)
    for head in range(0, heads, 2):
        base = head // 2 * pair_width
        even_nope = query_ref[:, base : base + nope_dim]
        even_rope = query_ref[:, base + nope_dim : base + nope_dim + 2 * rope_dim]
        odd_all = query_ref[:, base + nope_dim : base + pair_width]
        odd_rope = query_ref[:, base + pair_width - 2 * rope_dim : base + pair_width]
        odd_map = jnp.concatenate([pad, key_up_ref[first_head + head + 1], pad], axis=0)
        out_ref[head, :, :lat_dim] = jnp.dot(
            even_nope, key_up_ref[first_head + head], preferred_element_type=jnp.float32
        ).astype(out_ref.dtype)
        out_ref[head + 1, :, :lat_dim] = jnp.dot(
            odd_all, odd_map, preferred_element_type=jnp.float32
        ).astype(out_ref.dtype)
        zero = jnp.zeros_like(even_rope)
        out_ref[head, :, lat_dim:] = jnp.where(lane < rope_dim, even_rope, zero)
        out_ref[head + 1, :, lat_dim:] = jnp.where(lane >= rope_dim, odd_rope, zero)


def absorb(queries, key_up, rope_dim, heads):
    tokens = queries.shape[0]
    _, nope_dim, lat_dim = key_up.shape
    out_dim = lat_dim + 2 * rope_dim

    def kernel(query_ref, key_up_ref, out_ref):
        absorb_into(query_ref, key_up_ref, out_ref, 0, nope_dim, rope_dim)

    return pl.pallas_call(
        kernel,
        in_specs=[VMEM] * 2,
        out_specs=VMEM,
        out_shape=jax.ShapeDtypeStruct((heads, tokens, out_dim), queries.dtype),
        compiler_params=pltpu.CompilerParams(vmem_limit_bytes=12 << 20),
        cost_estimate=pl.CostEstimate(
            flops=2 * tokens * heads * nope_dim * lat_dim,
            bytes_accessed=2 * (queries.size + key_up.size + heads * tokens * out_dim),
            transcendentals=0,
        ),
    )(queries, key_up)


def load_keys(own_ref, mine_refs, other_refs, keys_ref, keys_t_ref):
    block = own_ref.shape[0]
    half = block // 2
    keys_ref[:block, :] = own_ref[...]
    mine = lax.axis_index("head") * half
    for slot in range(1, 4):
        first = pl.multiple_of(slot * block + mine, half)
        keys_ref[pl.ds(first, half), :] = mine_refs[slot - 1][...]
        first = pl.multiple_of(slot * block + half - mine, half)
        keys_ref[pl.ds(first, half), :] = other_refs[slot - 1][...]
    keys_t_ref[...] = keys_ref[...].T


def hide_of(start_ref, prefix_ref, slot, first_token, tokens, block, context):
    here = lax.axis_index("seq")
    there = lax.bitwise_xor(here, slot)
    span_blocks = context // block // NSPAN
    span_first = start_ref[there // span_blocks]
    prefix = prefix_ref[there // span_blocks]
    first_pos = span_first + there % span_blocks * block + first_token
    column = lax.broadcasted_iota(jnp.int32, (tokens, context), 1)
    row = lax.broadcasted_iota(jnp.int32, (tokens, context), 0)
    position = lax.bitwise_xor(column // block, here) * block + column % block
    visible = (position < prefix) | ((position >= span_first) & (position <= row + first_pos))
    return jnp.where(visible, 0.0, masked_fill)


def attention(query, keys_ref, keys_t_ref, hide, softmax_scale, lat_dim):
    heads, tokens, width = query.shape
    context = keys_ref.shape[0]
    scores = jnp.dot(
        query.reshape(heads * tokens, width), keys_t_ref[...], preferred_element_type=jnp.float32
    )
    scores = scores.reshape(heads, tokens, context) + hide[None]
    peak = jnp.max(scores, axis=2, keepdims=True)
    weights = jnp.exp((scores - peak) * softmax_scale)
    inverse = 1.0 / jnp.sum(weights, axis=2, keepdims=True)
    rounded = weights.astype(keys_ref.dtype).reshape(heads * tokens, context)
    summed = jnp.dot(rounded, keys_ref[:, :lat_dim], preferred_element_type=jnp.float32)
    return (summed.reshape(heads, tokens, lat_dim) * inverse).astype(keys_ref.dtype)


def attend_heads(
    start_ref, prefix_ref, query_ref, value_up_ref, keys_ref, keys_t_ref, out_ref,
    softmax_scale, first_token, head_block,
):
    heads, block, _ = query_ref.shape
    tokens = out_ref.shape[0]
    _, lat_dim, value_dim = value_up_ref.shape
    hide = hide_of(start_ref, prefix_ref, 0, first_token, tokens, block, keys_ref.shape[0])
    for base in range(0, heads, head_block):
        latent_out = attention(
            query_ref[base : base + head_block, first_token : first_token + tokens, :],
            keys_ref, keys_t_ref, hide, softmax_scale, lat_dim,
        )
        for head in range(head_block):
            out_ref[:, (base + head) * value_dim : (base + head + 1) * value_dim] = jnp.dot(
                latent_out[head], value_up_ref[base + head], preferred_element_type=jnp.float32
            ).astype(out_ref.dtype)


def attend_kernel(
    start_ref, prefix_ref, query_ref, value_up_ref, *refs, softmax_scale, first_token, head_block
):
    if len(refs) > 3:
        own_ref, *received, out_ref, keys_ref, keys_t_ref = refs
        load_keys(own_ref, received[:3], received[3:], keys_ref, keys_t_ref)
    else:
        keys_ref, keys_t_ref, out_ref = refs
    attend_heads(
        start_ref, prefix_ref, query_ref, value_up_ref, keys_ref, keys_t_ref, out_ref,
        softmax_scale, first_token, head_block,
    )


def attend(spans, absorbed, keys, value_up, softmax_scale, first_token, tokens, context):
    heads, _, width = absorbed.shape
    _, lat_dim, value_dim = value_up.shape
    out_shape = [jax.ShapeDtypeStruct((tokens, heads * value_dim), absorbed.dtype)]
    if len(keys) > 2:
        out_shape.append(jax.ShapeDtypeStruct((context, width), absorbed.dtype))
        out_shape.append(jax.ShapeDtypeStruct((width, context), absorbed.dtype))
    return pl.pallas_call(
        functools.partial(
            attend_kernel,
            softmax_scale=softmax_scale,
            first_token=first_token,
            head_block=heads // 2,
        ),
        in_specs=[SMEM] * 2 + [VMEM] * (2 + len(keys)),
        out_specs=[VMEM] * len(out_shape),
        out_shape=out_shape,
        compiler_params=pltpu.CompilerParams(vmem_limit_bytes=24 << 20),
        cost_estimate=pl.CostEstimate(
            flops=2 * tokens * heads * (context * (width + lat_dim) + lat_dim * value_dim),
            bytes_accessed=2 * (heads * tokens * width + value_up.size + heads * tokens * value_dim),
            transcendentals=heads * tokens * context,
        ),
    )(*spans, absorbed, value_up, *keys)


def everywhere_kernel(
    start_ref, prefix_ref, query0_ref, query1_ref, query2_ref, query3_ref,
    keys_ref, keys_t_ref, key_up_ref, value_up_ref, out_ref,
    queries_ref, absorbed_ref, *, softmax_scale, rope_dim, first_head,
):
    tokens = query0_ref.shape[0]
    _, nope_dim, lat_dim = key_up_ref.shape
    value_dim = value_up_ref.shape[2]
    heads = absorbed_ref.shape[0]
    for slot, ref in enumerate((query0_ref, query1_ref, query2_ref, query3_ref)):
        queries_ref[slot * tokens : (slot + 1) * tokens, :] = ref[...]
    absorb_into(queries_ref, key_up_ref, absorbed_ref, first_head, nope_dim, rope_dim)
    for slot in range(4):
        rows = slice(slot * tokens, (slot + 1) * tokens)
        latent_out = attention(
            absorbed_ref[:, rows, :], keys_ref, keys_t_ref,
            hide_of(start_ref, prefix_ref, slot, 0, tokens, tokens, keys_ref.shape[0]),
            softmax_scale, lat_dim,
        )
        for head in range(heads):
            out_ref[rows, head * value_dim : (head + 1) * value_dim] = jnp.dot(
                latent_out[head], value_up_ref[first_head + head],
                preferred_element_type=jnp.float32,
            ).astype(out_ref.dtype)


def attend_everywhere(spans, query_slots, keys, key_up, value_up, softmax_scale, rope_dim):
    tokens, width = query_slots[0].shape
    heads = width // (key_up.shape[1] + rope_dim)
    _, lat_dim, value_dim = value_up.shape
    context, key_width = keys[0].shape
    return pl.pallas_call(
        functools.partial(
            everywhere_kernel,
            softmax_scale=softmax_scale,
            rope_dim=rope_dim,
            first_head=key_up.shape[0] - heads,
        ),
        in_specs=[SMEM] * 2 + [VMEM] * 8,
        out_specs=VMEM,
        scratch_shapes=[
            pltpu.VMEM((4 * tokens, width), key_up.dtype),
            pltpu.VMEM((heads, 4 * tokens, key_width), key_up.dtype),
        ],
        out_shape=jax.ShapeDtypeStruct((4 * tokens, heads * value_dim), key_up.dtype),
        compiler_params=pltpu.CompilerParams(vmem_limit_bytes=24 << 20),
        cost_estimate=pl.CostEstimate(
            flops=8 * tokens * heads * (context * (key_width + lat_dim) + 2 * lat_dim * value_dim),
            bytes_accessed=8 * tokens * (width + heads * value_dim),
            transcendentals=4 * heads * tokens * context,
        ),
    )(*spans, *query_slots, *keys, key_up, value_up)


def project_kernel(
    own_ref, near_ref, far_ref, cross_ref, everywhere_ref, weight_ref, keep_ref, send_ref,
    rows_ref, sums_ref, *, first_token, first_column,
):
    tokens, split = own_ref.shape
    block = everywhere_ref.shape[0] // 4
    columns = keep_ref.shape[1]
    column_block = sums_ref.shape[2]
    for slot, ref in enumerate((own_ref, near_ref, far_ref, cross_ref)):
        rows = slice(slot * tokens, (slot + 1) * tokens)
        first = slot * block + first_token
        rows_ref[rows, :split] = ref[...]
        rows_ref[rows, split:] = everywhere_ref[first : first + tokens, :]
    here = lax.axis_index("seq")
    parity = here % 2
    kept = jnp.where(here // 2 == lax.axis_index("head"), 0, 2)
    for base in range(0, columns, column_block):
        product = jnp.dot(
            rows_ref[...],
            weight_ref[:, first_column + base : first_column + base + column_block],
            preferred_element_type=jnp.float32,
        )
        sums_ref[...] = product.reshape(sums_ref.shape)
        for part in range(2):
            offset = parity if part == 0 else 1 - parity
            rows = slice(part * tokens, (part + 1) * tokens)
            target = slice(base, base + column_block)
            keep_ref[rows, target] = sums_ref[kept + offset]
            send_ref[rows, target] = sums_ref[2 - kept + offset].astype(send_ref.dtype)


def project(slots, everywhere, weight, first_token, first_column, columns, column_block):
    tokens = slots[0].shape[0]
    depth = weight.shape[0]
    return pl.pallas_call(
        functools.partial(project_kernel, first_token=first_token, first_column=first_column),
        in_specs=[VMEM] * 6,
        out_specs=[VMEM] * 2,
        scratch_shapes=[
            pltpu.VMEM((4 * tokens, depth), weight.dtype),
            pltpu.VMEM((4, tokens, column_block), jnp.float32),
        ],
        out_shape=[
            jax.ShapeDtypeStruct((2 * tokens, columns), jnp.float32),
            jax.ShapeDtypeStruct((2 * tokens, columns), weight.dtype),
        ],
        compiler_params=pltpu.CompilerParams(vmem_limit_bytes=12 << 20),
        cost_estimate=pl.CostEstimate(
            flops=8 * tokens * depth * columns,
            bytes_accessed=2 * (depth * columns + 4 * tokens * depth + 6 * tokens * columns),
            transcendentals=0,
        ),
    )(*slots, everywhere, weight)


def finish_kernel(*refs, firsts, aliased):
    count = len(firsts)
    out_ref, sums_ref, sems = refs[-3:]
    refs = refs[aliased : aliased + 2 * count]
    half = out_ref.shape[0] // 2
    copies = []
    done = 0
    for index, first in enumerate(firsts):
        keep_ref, came_ref = refs[index], refs[count + index]
        tokens = keep_ref.shape[0] // 2
        for part in range(2):
            rows = slice(part * tokens, (part + 1) * tokens)
            sums_ref[done + part * tokens : done + (part + 1) * tokens, :] = (
                keep_ref[rows, :] + came_ref[rows, :].astype(jnp.float32)
            ).astype(sums_ref.dtype)
            copies.append(
                pltpu.make_async_copy(
                    sums_ref.at[pl.ds(done + part * tokens, tokens), :],
                    out_ref.at[pl.ds(part * half + first, tokens), :],
                    sems.at[2 * index + part],
                )
            )
            copies[-1].start()
        done += 2 * tokens
    for copy in copies:
        copy.wait()


def finish(partial, kept, came, firsts, rows):
    columns = kept[0].shape[1]
    before = [] if partial is None else [partial]
    return pl.pallas_call(
        functools.partial(finish_kernel, firsts=firsts, aliased=len(before)),
        in_specs=[pl.BlockSpec(memory_space=pl.ANY)] * len(before) + [VMEM] * (2 * len(kept)),
        out_specs=pl.BlockSpec(memory_space=pl.ANY),
        scratch_shapes=[
            pltpu.VMEM((sum(keep.shape[0] for keep in kept), columns), came[0].dtype),
            pltpu.SemaphoreType.DMA((2 * len(kept),)),
        ],
        out_shape=jax.ShapeDtypeStruct((rows, columns), came[0].dtype),
        input_output_aliases={0: 0} if before else {},
        compiler_params=pltpu.CompilerParams(vmem_limit_bytes=4 << 20),
        cost_estimate=pl.CostEstimate(
            flops=sum(keep.size for keep in kept),
            bytes_accessed=8 * sum(keep.size for keep in kept),
            transcendentals=0,
        ),
    )(*before, *kept, *came)


def on_device_pairs(
    q_heads, cache_latent, cache_rope, span_start, prefix_len, key_up, value_up, out_weight
):
    queries = q_heads[0]
    tokens = queries.shape[0]
    head_count, nope_dim = key_up.shape[1:3]
    rope_dim = cache_rope.shape[2]
    head_width = nope_dim + rope_dim
    softmax_scale = head_width ** (-0.5)
    columns = out_weight.shape[2]
    everywhere_heads = head_count // EVERYWHERE_SHARE
    sent_heads = head_count - everywhere_heads
    context = tokens * lax.axis_size("seq")
    spans = (span_start[0], prefix_len[0])
    sizes = [tokens * share // sum(SHARES) for share in SHARES]
    firsts = [sum(sizes[:index]) for index in range(CHUNKS)]
    own, half = prepare(
        pltpu.with_memory_space_constraint(cache_latent[0], pltpu.HBM),
        pltpu.with_memory_space_constraint(cache_rope[0].T, pltpu.HBM),
    )
    far = exchange(half, "seq", 2)
    near = exchange(half, "seq", 1)
    absorbed = absorb(queries, key_up[0], rope_dim, sent_heads)
    cross = exchange(far, "seq", 1)
    near_x = exchange(near, "head", 1)
    far_x = exchange(far, "head", 1)
    cross_x = exchange(cross, "head", 1)
    keys = [own, near, far, cross, near_x, far_x, cross_x]
    own = queries[:, sent_heads * head_width :]
    far = exchange(own, "seq", 2)
    near = exchange(own, "seq", 1)
    cross = exchange(far, "seq", 1)
    query_slots = [own, near, far, cross]
    parts = []
    for index in range(CHUNKS):
        own, *rest = attend(
            spans, absorbed, keys, value_up[0], softmax_scale, firsts[index],
            sizes[index], context,
        )
        keys = rest or keys
        far = exchange(own, "seq", 2)
        near = exchange(own, "seq", 1)
        if DIRECT[index]:
            cross = exchange(own, "seq", 3)
        else:
            cross = exchange(far, "seq", 1)
        parts.append([own, near, far, cross])
    everywhere = attend_everywhere(
        spans, query_slots, keys, key_up[0], value_up[0], softmax_scale, rope_dim
    )
    kept, came = [], []
    for index, slots in enumerate(parts):
        keep, sent = project(
            slots, everywhere, out_weight[0], firsts[index], 0, columns, columns // 2
        )
        kept.append(keep)
        came.append(exchange(sent, "head", 1))
    out = finish(None, kept[:-1], came[:-1], firsts[:-1], 2 * tokens)
    out = finish(out, kept[-1:], came[-1:], firsts[-1:], 2 * tokens)
    return out[None]


def on_device_any(
    q_heads, cache_latent, cache_rope, span_start, prefix_len, key_up, value_up, out_weight
):
    queries_flat = q_heads[0]
    tokens = queries_flat.shape[0]
    head_count = key_up.shape[1]
    nope_dim = key_up.shape[2]
    head_width = queries_flat.shape[1] // head_count
    seq_count = lax.axis_size("seq")
    seq_index = lax.axis_index("seq")
    queries = queries_flat.reshape(tokens, head_count, head_width)
    absorbed = jnp.einsum(
        "thn,hnl->thl", queries[:, :, :nope_dim], key_up[0], preferred_element_type=jnp.float32
    ).astype(jnp.bfloat16)
    rope_query = queries[:, :, nope_dim:]
    softmax_scale = head_width ** (-0.5)
    span_len = tokens * seq_count // NSPAN
    global_row = seq_index * tokens + jnp.arange(tokens, dtype=jnp.int32)
    one_hot = (global_row // span_len)[:, None] == jnp.arange(NSPAN, dtype=jnp.int32)[None, :]
    span_first = jnp.sum(jnp.where(one_hot, span_start[0][None, :], 0), axis=1)
    prefix_row = jnp.sum(jnp.where(one_hot, prefix_len[0][None, :], 0), axis=1)
    token_pos = span_first + global_row % span_len
    latent = lax.all_gather(cache_latent[0], "seq", axis=0, tiled=True)
    rope = lax.all_gather(cache_rope[0], "seq", axis=0, tiled=True)
    key_pos = jnp.arange(latent.shape[0], dtype=jnp.int32)
    visible = (
        (key_pos[None, :] < prefix_row[:, None])
        | (key_pos[None, :] >= span_first[:, None]) & (key_pos[None, :] <= token_pos[:, None])
    )[:, None, :]
    scores = jnp.einsum(
        "thl,kl->thk", absorbed, latent, preferred_element_type=jnp.float32
    ) + jnp.einsum("thr,kr->thk", rope_query, rope, preferred_element_type=jnp.float32)
    scores = jnp.where(visible, scores * softmax_scale, masked_fill)
    peak = jnp.max(scores, axis=2, keepdims=True)
    weights = jnp.where(visible, jnp.exp(scores - peak), 0.0)
    totals = jnp.sum(weights, axis=2)
    summed = jnp.einsum(
        "thk,kl->thl", weights.astype(jnp.bfloat16), latent, preferred_element_type=jnp.float32
    )
    latent_out = (summed / totals[:, :, None]).astype(jnp.bfloat16)
    head_out = (
        jnp.einsum("thl,hlv->thv", latent_out, value_up[0], preferred_element_type=jnp.float32)
        .astype(jnp.bfloat16)
        .reshape(tokens, -1)
    )
    partial_out = jnp.dot(
        lax.all_gather(head_out, "seq", axis=0, tiled=True),
        out_weight[0],
        preferred_element_type=jnp.float32,
    )
    mixed_out = lax.psum_scatter(partial_out, "head", scatter_dimension=0, tiled=True)
    return mixed_out.astype(jnp.bfloat16)[None]


def solution(mesh):
    in_specs = (
        P("section", ("groups", "seq"), "head"),
        P("section", ("groups", "seq"), None),
        P("section", ("groups", "seq"), None),
        P("section", "groups"),
        P("section", "groups"),
        P("section", "head", None, None),
        P("section", "head", None, None),
        P("section", "head", "seq"),
    )
    out_specs = P("section", ("groups", "head"), "seq")
    paired = mesh.shape["seq"] == 4 and mesh.shape["head"] == 2
    return jax.shard_map(
        on_device_pairs if paired else on_device_any,
        mesh=mesh, in_specs=in_specs, out_specs=out_specs, check_vma=False,
    )
```

```python
import functools

import jax
import jax.numpy as jnp
from jax import lax
from jax.experimental import pallas as pl
from jax.experimental.pallas import tpu as pltpu
from jax.sharding import PartitionSpec as P


NSPAN = 2

SHARES = (2, 2, 2, 2)
CHUNKS = len(SHARES)
PREPARE_FLOPS = 10_000_000_000
EVERYWHERE_SHARE = 8
DIRECT = (False, False, False, False)

masked_fill = -1e30

VMEM = pl.BlockSpec(memory_space=pltpu.VMEM)
SMEM = pl.BlockSpec(memory_space=pltpu.SMEM)


def exchange(value, axis, distance):
    count = lax.axis_size(axis)
    return lax.ppermute(value, axis, [(i, i ^ distance) for i in range(count)])


def prepare_kernel(latent_ref, rope_ref, keys_ref, half_ref, loaded_ref, sems):
    lat_dim = latent_ref.shape[1]
    half = half_ref.shape[0]
    latent_copy = pltpu.make_async_copy(latent_ref, keys_ref.at[:, :lat_dim], sems.at[0])
    rope_copy = pltpu.make_async_copy(rope_ref, loaded_ref, sems.at[1])
    latent_copy.start()
    rope_copy.start()
    rope_copy.wait()
    keys_ref[:, lat_dim:] = jnp.concatenate([loaded_ref[...]] * 2, axis=0).T
    latent_copy.wait()
    first = pl.multiple_of(lax.axis_index("head") * half, half)
    half_ref[...] = keys_ref[pl.ds(first, half), :]


def prepare(latent, rope):
    tokens, lat_dim = latent.shape
    rope_dim = rope.shape[0]
    width = lat_dim + 2 * rope_dim
    return pl.pallas_call(
        prepare_kernel,
        in_specs=[pl.BlockSpec(memory_space=pl.ANY)] * 2,
        out_specs=[VMEM] * 2,
        scratch_shapes=[
            pltpu.VMEM((rope_dim, tokens), rope.dtype),
            pltpu.SemaphoreType.DMA((2,)),
        ],
        out_shape=[
            jax.ShapeDtypeStruct((tokens, width), latent.dtype),
            jax.ShapeDtypeStruct((tokens // 2, width), latent.dtype),
        ],
        compiler_params=pltpu.CompilerParams(vmem_limit_bytes=2 << 20),
        cost_estimate=pl.CostEstimate(
            flops=PREPARE_FLOPS, bytes_accessed=4 * latent.size, transcendentals=0
        ),
    )(latent, rope)


def absorb_into(query_ref, key_up_ref, out_ref, first_head, nope_dim, rope_dim):
    heads, tokens, _ = out_ref.shape
    lat_dim = key_up_ref.shape[2]
    pair_width = 2 * (nope_dim + rope_dim)
    lane = lax.broadcasted_iota(jnp.int32, (tokens, 2 * rope_dim), 1)
    pad = jnp.zeros((rope_dim, lat_dim), key_up_ref.dtype)
    for head in range(0, heads, 2):
        base = head // 2 * pair_width
        even_nope = query_ref[:, base : base + nope_dim]
        even_rope = query_ref[:, base + nope_dim : base + nope_dim + 2 * rope_dim]
        odd_all = query_ref[:, base + nope_dim : base + pair_width]
        odd_rope = query_ref[:, base + pair_width - 2 * rope_dim : base + pair_width]
        odd_map = jnp.concatenate([pad, key_up_ref[first_head + head + 1], pad], axis=0)
        out_ref[head, :, :lat_dim] = jnp.dot(
            even_nope, key_up_ref[first_head + head], preferred_element_type=jnp.float32
        ).astype(out_ref.dtype)
        out_ref[head + 1, :, :lat_dim] = jnp.dot(
            odd_all, odd_map, preferred_element_type=jnp.float32
        ).astype(out_ref.dtype)
        zero = jnp.zeros_like(even_rope)
        out_ref[head, :, lat_dim:] = jnp.where(lane < rope_dim, even_rope, zero)
        out_ref[head + 1, :, lat_dim:] = jnp.where(lane >= rope_dim, odd_rope, zero)


def absorb(queries, key_up, rope_dim, heads):
    tokens = queries.shape[0]
    _, nope_dim, lat_dim = key_up.shape
    out_dim = lat_dim + 2 * rope_dim

    def kernel(query_ref, key_up_ref, out_ref):
        absorb_into(query_ref, key_up_ref, out_ref, 0, nope_dim, rope_dim)

    return pl.pallas_call(
        kernel,
        in_specs=[VMEM] * 2,
        out_specs=VMEM,
        out_shape=jax.ShapeDtypeStruct((heads, tokens, out_dim), queries.dtype),
        compiler_params=pltpu.CompilerParams(vmem_limit_bytes=12 << 20),
        cost_estimate=pl.CostEstimate(
            flops=2 * tokens * heads * nope_dim * lat_dim,
            bytes_accessed=2 * (queries.size + key_up.size + heads * tokens * out_dim),
            transcendentals=0,
        ),
    )(queries, key_up)


def load_keys(own_ref, mine_refs, other_refs, keys_ref, keys_t_ref):
    block = own_ref.shape[0]
    half = block // 2
    keys_ref[:block, :] = own_ref[...]
    mine = lax.axis_index("head") * half
    for slot in range(1, 4):
        first = pl.multiple_of(slot * block + mine, half)
        keys_ref[pl.ds(first, half), :] = mine_refs[slot - 1][...]
        first = pl.multiple_of(slot * block + half - mine, half)
        keys_ref[pl.ds(first, half), :] = other_refs[slot - 1][...]
    keys_t_ref[...] = keys_ref[...].T


def hide_of(start_ref, prefix_ref, slot, first_token, tokens, block, context):
    here = lax.axis_index("seq")
    there = lax.bitwise_xor(here, slot)
    span_blocks = context // block // NSPAN
    span_first = start_ref[there // span_blocks]
    prefix = prefix_ref[there // span_blocks]
    first_pos = span_first + there % span_blocks * block + first_token
    column = lax.broadcasted_iota(jnp.int32, (tokens, context), 1)
    row = lax.broadcasted_iota(jnp.int32, (tokens, context), 0)
    position = lax.bitwise_xor(column // block, here) * block + column % block
    visible = (position < prefix) | ((position >= span_first) & (position <= row + first_pos))
    return jnp.where(visible, 0.0, masked_fill)


def attention(query, keys_ref, keys_t_ref, hide, softmax_scale, lat_dim):
    heads, tokens, width = query.shape
    context = keys_ref.shape[0]
    scores = jnp.dot(
        query.reshape(heads * tokens, width), keys_t_ref[...], preferred_element_type=jnp.float32
    )
    scores = scores.reshape(heads, tokens, context) + hide[None]
    peak = jnp.max(scores, axis=2, keepdims=True)
    weights = jnp.exp((scores - peak) * softmax_scale)
    inverse = 1.0 / jnp.sum(weights, axis=2, keepdims=True)
    rounded = weights.astype(keys_ref.dtype).reshape(heads * tokens, context)
    summed = jnp.dot(rounded, keys_ref[:, :lat_dim], preferred_element_type=jnp.float32)
    return (summed.reshape(heads, tokens, lat_dim) * inverse).astype(keys_ref.dtype)


def attend_heads(
    start_ref, prefix_ref, query_ref, value_up_ref, keys_ref, keys_t_ref, out_ref,
    softmax_scale, first_token, head_block,
):
    heads, block, _ = query_ref.shape
    tokens = out_ref.shape[0]
    _, lat_dim, value_dim = value_up_ref.shape
    hide = hide_of(start_ref, prefix_ref, 0, first_token, tokens, block, keys_ref.shape[0])
    for base in range(0, heads, head_block):
        latent_out = attention(
            query_ref[base : base + head_block, first_token : first_token + tokens, :],
            keys_ref, keys_t_ref, hide, softmax_scale, lat_dim,
        )
        for head in range(head_block):
            out_ref[:, (base + head) * value_dim : (base + head + 1) * value_dim] = jnp.dot(
                latent_out[head], value_up_ref[base + head], preferred_element_type=jnp.float32
            ).astype(out_ref.dtype)


def attend_kernel(
    start_ref, prefix_ref, query_ref, value_up_ref, *refs, softmax_scale, first_token, head_block
):
    if len(refs) > 3:
        own_ref, *received, out_ref, keys_ref, keys_t_ref = refs
        load_keys(own_ref, received[:3], received[3:], keys_ref, keys_t_ref)
    else:
        keys_ref, keys_t_ref, out_ref = refs
    attend_heads(
        start_ref, prefix_ref, query_ref, value_up_ref, keys_ref, keys_t_ref, out_ref,
        softmax_scale, first_token, head_block,
    )


def attend(spans, absorbed, keys, value_up, softmax_scale, first_token, tokens, context):
    heads, _, width = absorbed.shape
    _, lat_dim, value_dim = value_up.shape
    out_shape = [jax.ShapeDtypeStruct((tokens, heads * value_dim), absorbed.dtype)]
    if len(keys) > 2:
        out_shape.append(jax.ShapeDtypeStruct((context, width), absorbed.dtype))
        out_shape.append(jax.ShapeDtypeStruct((width, context), absorbed.dtype))
    return pl.pallas_call(
        functools.partial(
            attend_kernel,
            softmax_scale=softmax_scale,
            first_token=first_token,
            head_block=heads // 2,
        ),
        in_specs=[SMEM] * 2 + [VMEM] * (2 + len(keys)),
        out_specs=[VMEM] * len(out_shape),
        out_shape=out_shape,
        compiler_params=pltpu.CompilerParams(vmem_limit_bytes=24 << 20),
        cost_estimate=pl.CostEstimate(
            flops=2 * tokens * heads * (context * (width + lat_dim) + lat_dim * value_dim),
            bytes_accessed=2 * (heads * tokens * width + value_up.size + heads * tokens * value_dim),
            transcendentals=heads * tokens * context,
        ),
    )(*spans, absorbed, value_up, *keys)


def everywhere_kernel(
    start_ref, prefix_ref, query0_ref, query1_ref, query2_ref, query3_ref,
    keys_ref, keys_t_ref, key_up_ref, value_up_ref, out_ref,
    queries_ref, absorbed_ref, *, softmax_scale, rope_dim, first_head,
):
    tokens = query0_ref.shape[0]
    _, nope_dim, lat_dim = key_up_ref.shape
    value_dim = value_up_ref.shape[2]
    heads = absorbed_ref.shape[0]
    for slot, ref in enumerate((query0_ref, query1_ref, query2_ref, query3_ref)):
        queries_ref[slot * tokens : (slot + 1) * tokens, :] = ref[...]
    absorb_into(queries_ref, key_up_ref, absorbed_ref, first_head, nope_dim, rope_dim)
    for slot in range(4):
        rows = slice(slot * tokens, (slot + 1) * tokens)
        latent_out = attention(
            absorbed_ref[:, rows, :], keys_ref, keys_t_ref,
            hide_of(start_ref, prefix_ref, slot, 0, tokens, tokens, keys_ref.shape[0]),
            softmax_scale, lat_dim,
        )
        for head in range(heads):
            out_ref[rows, head * value_dim : (head + 1) * value_dim] = jnp.dot(
                latent_out[head], value_up_ref[first_head + head],
                preferred_element_type=jnp.float32,
            ).astype(out_ref.dtype)


def attend_everywhere(spans, query_slots, keys, key_up, value_up, softmax_scale, rope_dim):
    tokens, width = query_slots[0].shape
    heads = width // (key_up.shape[1] + rope_dim)
    _, lat_dim, value_dim = value_up.shape
    context, key_width = keys[0].shape
    return pl.pallas_call(
        functools.partial(
            everywhere_kernel,
            softmax_scale=softmax_scale,
            rope_dim=rope_dim,
            first_head=key_up.shape[0] - heads,
        ),
        in_specs=[SMEM] * 2 + [VMEM] * 8,
        out_specs=VMEM,
        scratch_shapes=[
            pltpu.VMEM((4 * tokens, width), key_up.dtype),
            pltpu.VMEM((heads, 4 * tokens, key_width), key_up.dtype),
        ],
        out_shape=jax.ShapeDtypeStruct((4 * tokens, heads * value_dim), key_up.dtype),
        compiler_params=pltpu.CompilerParams(vmem_limit_bytes=24 << 20),
        cost_estimate=pl.CostEstimate(
            flops=8 * tokens * heads * (context * (key_width + lat_dim) + 2 * lat_dim * value_dim),
            bytes_accessed=8 * tokens * (width + heads * value_dim),
            transcendentals=4 * heads * tokens * context,
        ),
    )(*spans, *query_slots, *keys, key_up, value_up)


def project_kernel(
    own_ref, near_ref, far_ref, cross_ref, everywhere_ref, weight_ref, keep_ref, send_ref,
    rows_ref, sums_ref, *, first_token, first_column,
):
    tokens, split = own_ref.shape
    block = everywhere_ref.shape[0] // 4
    columns = keep_ref.shape[1]
    column_block = sums_ref.shape[2]
    for slot, ref in enumerate((own_ref, near_ref, far_ref, cross_ref)):
        rows = slice(slot * tokens, (slot + 1) * tokens)
        first = slot * block + first_token
        rows_ref[rows, :split] = ref[...]
        rows_ref[rows, split:] = everywhere_ref[first : first + tokens, :]
    here = lax.axis_index("seq")
    parity = here % 2
    kept = jnp.where(here // 2 == lax.axis_index("head"), 0, 2)
    for base in range(0, columns, column_block):
        product = jnp.dot(
            rows_ref[...],
            weight_ref[:, first_column + base : first_column + base + column_block],
            preferred_element_type=jnp.float32,
        )
        sums_ref[...] = product.reshape(sums_ref.shape)
        for part in range(2):
            offset = parity if part == 0 else 1 - parity
            rows = slice(part * tokens, (part + 1) * tokens)
            target = slice(base, base + column_block)
            keep_ref[rows, target] = sums_ref[kept + offset]
            send_ref[rows, target] = sums_ref[2 - kept + offset].astype(send_ref.dtype)


def project(slots, everywhere, weight, first_token, first_column, columns, column_block):
    tokens = slots[0].shape[0]
    depth = weight.shape[0]
    return pl.pallas_call(
        functools.partial(project_kernel, first_token=first_token, first_column=first_column),
        in_specs=[VMEM] * 6,
        out_specs=[VMEM] * 2,
        scratch_shapes=[
            pltpu.VMEM((4 * tokens, depth), weight.dtype),
            pltpu.VMEM((4, tokens, column_block), jnp.float32),
        ],
        out_shape=[
            jax.ShapeDtypeStruct((2 * tokens, columns), jnp.float32),
            jax.ShapeDtypeStruct((2 * tokens, columns), weight.dtype),
        ],
        compiler_params=pltpu.CompilerParams(vmem_limit_bytes=12 << 20),
        cost_estimate=pl.CostEstimate(
            flops=8 * tokens * depth * columns,
            bytes_accessed=2 * (depth * columns + 4 * tokens * depth + 6 * tokens * columns),
            transcendentals=0,
        ),
    )(*slots, everywhere, weight)


def finish_kernel(*refs, firsts, aliased):
    count = len(firsts)
    out_ref, sums_ref, sems = refs[-3:]
    refs = refs[aliased : aliased + 2 * count]
    half = out_ref.shape[0] // 2
    copies = []
    done = 0
    for index, first in enumerate(firsts):
        keep_ref, came_ref = refs[index], refs[count + index]
        tokens = keep_ref.shape[0] // 2
        sums_ref[done : done + 2 * tokens, :] = (
            keep_ref[...] + came_ref[...].astype(jnp.float32)
        ).astype(sums_ref.dtype)
        for part in range(2):
            copies.append(
                pltpu.make_async_copy(
                    sums_ref.at[pl.ds(done + part * tokens, tokens), :],
                    out_ref.at[pl.ds(part * half + first, tokens), :],
                    sems.at[2 * index + part],
                )
            )
            copies[-1].start()
        done += 2 * tokens
    for copy in copies:
        copy.wait()


def finish(partial, kept, came, firsts, rows):
    columns = kept[0].shape[1]
    before = [] if partial is None else [partial]
    return pl.pallas_call(
        functools.partial(finish_kernel, firsts=firsts, aliased=len(before)),
        in_specs=[pl.BlockSpec(memory_space=pl.ANY)] * len(before) + [VMEM] * (2 * len(kept)),
        out_specs=pl.BlockSpec(memory_space=pl.ANY),
        scratch_shapes=[
            pltpu.VMEM((sum(keep.shape[0] for keep in kept), columns), came[0].dtype),
            pltpu.SemaphoreType.DMA((2 * len(kept),)),
        ],
        out_shape=jax.ShapeDtypeStruct((rows, columns), came[0].dtype),
        input_output_aliases={0: 0} if before else {},
        compiler_params=pltpu.CompilerParams(vmem_limit_bytes=4 << 20),
        cost_estimate=pl.CostEstimate(
            flops=sum(keep.size for keep in kept),
            bytes_accessed=8 * sum(keep.size for keep in kept),
            transcendentals=0,
        ),
    )(*before, *kept, *came)


def on_device_pairs(
    q_heads, cache_latent, cache_rope, span_start, prefix_len, key_up, value_up, out_weight
):
    queries = q_heads[0]
    tokens = queries.shape[0]
    head_count, nope_dim = key_up.shape[1:3]
    rope_dim = cache_rope.shape[2]
    head_width = nope_dim + rope_dim
    softmax_scale = head_width ** (-0.5)
    columns = out_weight.shape[2]
    everywhere_heads = head_count // EVERYWHERE_SHARE
    sent_heads = head_count - everywhere_heads
    context = tokens * lax.axis_size("seq")
    spans = (span_start[0], prefix_len[0])
    sizes = [tokens * share // sum(SHARES) for share in SHARES]
    firsts = [sum(sizes[:index]) for index in range(CHUNKS)]
    own, half = prepare(
        pltpu.with_memory_space_constraint(cache_latent[0], pltpu.HBM),
        pltpu.with_memory_space_constraint(cache_rope[0].T, pltpu.HBM),
    )
    far = exchange(half, "seq", 2)
    near = exchange(half, "seq", 1)
    absorbed = absorb(queries, key_up[0], rope_dim, sent_heads)
    cross = exchange(far, "seq", 1)
    near_x = exchange(near, "head", 1)
    far_x = exchange(far, "head", 1)
    cross_x = exchange(cross, "head", 1)
    keys = [own, near, far, cross, near_x, far_x, cross_x]
    own = queries[:, sent_heads * head_width :]
    far = exchange(own, "seq", 2)
    near = exchange(own, "seq", 1)
    cross = exchange(far, "seq", 1)
    query_slots = [own, near, far, cross]
    parts = []
    for index in range(CHUNKS):
        own, *rest = attend(
            spans, absorbed, keys, value_up[0], softmax_scale, firsts[index],
            sizes[index], context,
        )
        keys = rest or keys
        far = exchange(own, "seq", 2)
        near = exchange(own, "seq", 1)
        if DIRECT[index]:
            cross = exchange(own, "seq", 3)
        else:
            cross = exchange(far, "seq", 1)
        parts.append([own, near, far, cross])
    everywhere = attend_everywhere(
        spans, query_slots, keys, key_up[0], value_up[0], softmax_scale, rope_dim
    )
    kept, came = [], []
    for index, slots in enumerate(parts):
        keep, sent = project(
            slots, everywhere, out_weight[0], firsts[index], 0, columns, columns // 2
        )
        kept.append(keep)
        came.append(exchange(sent, "head", 1))
    out = finish(None, kept[:-1], came[:-1], firsts[:-1], 2 * tokens)
    out = finish(out, kept[-1:], came[-1:], firsts[-1:], 2 * tokens)
    return out[None]


def on_device_any(
    q_heads, cache_latent, cache_rope, span_start, prefix_len, key_up, value_up, out_weight
):
    queries_flat = q_heads[0]
    tokens = queries_flat.shape[0]
    head_count = key_up.shape[1]
    nope_dim = key_up.shape[2]
    head_width = queries_flat.shape[1] // head_count
    seq_count = lax.axis_size("seq")
    seq_index = lax.axis_index("seq")
    queries = queries_flat.reshape(tokens, head_count, head_width)
    absorbed = jnp.einsum(
        "thn,hnl->thl", queries[:, :, :nope_dim], key_up[0], preferred_element_type=jnp.float32
    ).astype(jnp.bfloat16)
    rope_query = queries[:, :, nope_dim:]
    softmax_scale = head_width ** (-0.5)
    span_len = tokens * seq_count // NSPAN
    global_row = seq_index * tokens + jnp.arange(tokens, dtype=jnp.int32)
    one_hot = (global_row // span_len)[:, None] == jnp.arange(NSPAN, dtype=jnp.int32)[None, :]
    span_first = jnp.sum(jnp.where(one_hot, span_start[0][None, :], 0), axis=1)
    prefix_row = jnp.sum(jnp.where(one_hot, prefix_len[0][None, :], 0), axis=1)
    token_pos = span_first + global_row % span_len
    latent = lax.all_gather(cache_latent[0], "seq", axis=0, tiled=True)
    rope = lax.all_gather(cache_rope[0], "seq", axis=0, tiled=True)
    key_pos = jnp.arange(latent.shape[0], dtype=jnp.int32)
    visible = (
        (key_pos[None, :] < prefix_row[:, None])
        | (key_pos[None, :] >= span_first[:, None]) & (key_pos[None, :] <= token_pos[:, None])
    )[:, None, :]
    scores = jnp.einsum(
        "thl,kl->thk", absorbed, latent, preferred_element_type=jnp.float32
    ) + jnp.einsum("thr,kr->thk", rope_query, rope, preferred_element_type=jnp.float32)
    scores = jnp.where(visible, scores * softmax_scale, masked_fill)
    peak = jnp.max(scores, axis=2, keepdims=True)
    weights = jnp.where(visible, jnp.exp(scores - peak), 0.0)
    totals = jnp.sum(weights, axis=2)
    summed = jnp.einsum(
        "thk,kl->thl", weights.astype(jnp.bfloat16), latent, preferred_element_type=jnp.float32
    )
    latent_out = (summed / totals[:, :, None]).astype(jnp.bfloat16)
    head_out = (
        jnp.einsum("thl,hlv->thv", latent_out, value_up[0], preferred_element_type=jnp.float32)
        .astype(jnp.bfloat16)
        .reshape(tokens, -1)
    )
    partial_out = jnp.dot(
        lax.all_gather(head_out, "seq", axis=0, tiled=True),
        out_weight[0],
        preferred_element_type=jnp.float32,
    )
    mixed_out = lax.psum_scatter(partial_out, "head", scatter_dimension=0, tiled=True)
    return mixed_out.astype(jnp.bfloat16)[None]


def solution(mesh):
    in_specs = (
        P("section", ("groups", "seq"), "head"),
        P("section", ("groups", "seq"), None),
        P("section", ("groups", "seq"), None),
        P("section", "groups"),
        P("section", "groups"),
        P("section", "head", None, None),
        P("section", "head", None, None),
        P("section", "head", "seq"),
    )
    out_specs = P("section", ("groups", "head"), "seq")
    paired = mesh.shape["seq"] == 4 and mesh.shape["head"] == 2
    return jax.shard_map(
        on_device_pairs if paired else on_device_any,
        mesh=mesh, in_specs=in_specs, out_specs=out_specs, check_vma=False,
    )
```
